256 devices in a mesh: row: 16 (over z_hi, y), col: 16 (over z_lo, x, core).
Axes of the slice: x: 4, y: 4, z: 8 (z_hi: 4, z_lo: 2; z = z_hi * 2 + z_lo), core: 2. Of those that a mesh axis runs over, the one named last changes fastest.
Arguments:
- right_side: float32 [16, 16, 1024, 256], P('row', 'col'), may hold values from -4 to 4
- local_operator: bfloat16 [16, 16, 1536, 1536], P('row', 'col'), may hold values from -1 to 4
- local_inverse: bfloat16 [16, 16, 1536, 1536], P('row', 'col'), may hold values from -1 to 1
- coarse_basis: bfloat16 [16, 16, 1536, 32], P('row', 'col'), may hold values from -1 to 1
- coarse_inverse: bfloat16 [16, 512, 8192], P(None, 'col', 'row'), may hold values from -1 to 1
- send_rows: int32 [16, 16, 4, 128], P('row', 'col'), may hold values from 0 to 1023, as said below
- send_count: int32 [16, 16, 4], P('row', 'col'), may hold values from 0 to 128, as said below
Outputs:
- solution: float32 [16, 16, 1024, 256], P('row', 'col')
The draws below stay inside these ranges and needn't reach their ends.
Inputs may be any that keep to these rules, and one draw needn't show every extreme that they name: `send_rows`: within one subdomain and direction the entries are distinct owned rows; entries at or past that direction's count are ignored. `send_count`: 0 exactly where the neighbour in that direction lies outside the grid of subdomains; otherwise from 128 // 4 to 128, and 128 is reached.
All inputs are finite; a program needn't handle non-finite values.
Results may differ from the reference program's by a relative error of at most 0.023.
Values may be sent and summed in bfloat16 or wider, within the bound.
A program may use at most 64 MiB of HBM per device.

```python
import jax
import jax.numpy as jnp
from jax import lax

OWN = 1024
TILE = 128
COARSE = 32
RHS = 256
ITERS = 3
LOCAL = 1536
COARSE_ALL = 8192
N_ROW = 16
N_COL = 16


def draw_right_side(key, part):
    values = jnp.clip(jax.random.normal(key, (N_ROW, N_COL, OWN, RHS), jnp.float32), -4.0, 4.0)
    return values.astype(jnp.float32)


def dominant_matrix(key, low, high, spread):
    first, second = jax.random.split(jax.random.fold_in(key, 11))
    noise = jnp.clip(jax.random.normal(first, (N_ROW, N_COL, LOCAL, LOCAL), jnp.float32), -4.0, 4.0)
    diagonal = jnp.exp(jax.random.uniform(second, (N_ROW, N_COL, LOCAL), jnp.float32, jnp.log(low), jnp.log(high)))
    index_rows = lax.broadcasted_iota(jnp.int32, (LOCAL, LOCAL), 0)
    index_cols = lax.broadcasted_iota(jnp.int32, (LOCAL, LOCAL), 1)
    identity = (index_rows == index_cols).astype(jnp.float32)
    return noise * (spread / jnp.sqrt(1.0 * LOCAL)) + identity * diagonal[..., None]


def draw_local_operator(key, part):
    return dominant_matrix(key, 1.0, 3.0, 0.6).astype(jnp.bfloat16)


def draw_local_inverse(key, part):
    return dominant_matrix(jax.random.fold_in(key, 5), 0.3, 0.8, 0.3).astype(jnp.bfloat16)


def draw_coarse_basis(key, part):
    values = jnp.clip(jax.random.normal(jax.random.fold_in(key, 7), (N_ROW, N_COL, LOCAL, COARSE), jnp.float32), -4.0, 4.0)
    return (values * (1.0 * LOCAL * COARSE) ** (-0.25)).astype(jnp.bfloat16)


def draw_coarse_inverse(key, part):
    shape = (N_ROW, N_COL * COARSE, COARSE_ALL)
    noise = jnp.clip(jax.random.normal(jax.random.fold_in(key, 9), shape, jnp.float32), -4.0, 4.0)
    major = lax.broadcasted_iota(jnp.int32, shape, 0)
    minor = lax.broadcasted_iota(jnp.int32, shape, 1)
    column = lax.broadcasted_iota(jnp.int32, shape, 2)
    identity = (major * (N_COL * COARSE) + minor == column).astype(jnp.float32)
    return (noise / jnp.sqrt(1.0 * COARSE_ALL) + 0.3 * identity).astype(jnp.bfloat16)


def draw_send_rows(key, part):
    keys = jax.random.split(jax.random.fold_in(key, 13), N_ROW * N_COL * 4)
    chosen = jax.vmap(lambda single: jax.random.permutation(single, OWN)[:TILE])(keys)
    return chosen.reshape(N_ROW, N_COL, 4, TILE).astype(jnp.int32)


def draw_send_count(key, part):
    drawn = jax.random.randint(jax.random.fold_in(key, 17), (N_ROW, N_COL, 4), TILE // 4, TILE + 1).astype(jnp.int32)
    major = lax.broadcasted_iota(jnp.int32, (N_ROW, N_COL, 4), 0)
    minor = lax.broadcasted_iota(jnp.int32, (N_ROW, N_COL, 4), 1)
    direction = lax.broadcasted_iota(jnp.int32, (N_ROW, N_COL, 4), 2)
    outside = (direction == 0) & (major == 0) | (direction == 1) & (major == N_ROW - 1)
    outside = outside | (direction == 2) & (minor == 0) | (direction == 3) & (minor == N_COL - 1)
    forced = (direction == 1) & (major == 0) & (minor == 0)
    drawn = jnp.where(forced, TILE, drawn)
    return jnp.where(outside, 0, drawn).astype(jnp.int32)


def setup_inputs(seed: int = 0) -> dict:
    key_list = jax.random.split(jax.random.key(seed), 8)
    right_side = draw_right_side(jax.random.fold_in(key_list[7], 71), 0)
    local_operator = draw_local_operator(jax.random.fold_in(key_list[7], 71), 0)
    local_inverse = draw_local_inverse(jax.random.fold_in(key_list[7], 71), 0)
    coarse_basis = draw_coarse_basis(jax.random.fold_in(key_list[7], 71), 0)
    coarse_inverse = draw_coarse_inverse(jax.random.fold_in(key_list[7], 71), 0)
    send_rows = draw_send_rows(jax.random.fold_in(key_list[7], 71), 0)
    send_count = draw_send_count(jax.random.fold_in(key_list[7], 71), 0)
    return dict(right_side=right_side, local_operator=local_operator, local_inverse=local_inverse, coarse_basis=coarse_basis, coarse_inverse=coarse_inverse, send_rows=send_rows, send_count=send_count)


DAMPING = 0.5


def pack_tiles(values_half, send_rows, live_mask):
    picked = jax.vmap(jax.vmap(lambda rows_all, index_rows: rows_all[index_rows]))(values_half, send_rows)
    return picked * live_mask[..., None].astype(jnp.bfloat16)


def ghost_trade(buffer):
    zero_row = jnp.zeros_like(buffer[:1, :, 0])
    zero_col = jnp.zeros_like(buffer[:, :1, 0])
    from_lower_row = jnp.concatenate([zero_row, buffer[:-1, :, 1]], axis=0)
    from_upper_row = jnp.concatenate([buffer[1:, :, 0], zero_row], axis=0)
    from_lower_col = jnp.concatenate([zero_col, buffer[:, :-1, 3]], axis=1)
    from_upper_col = jnp.concatenate([buffer[:, 1:, 2], zero_col], axis=1)
    return jnp.stack([from_lower_row, from_upper_row, from_lower_col, from_upper_col], axis=2)


def with_ghosts(values_half, send_rows, live_mask):
    ghosts = ghost_trade(pack_tiles(values_half, send_rows, live_mask))
    dims = ghosts.shape
    flat_ghosts = ghosts.reshape(dims[0], dims[1], dims[2] * dims[3], dims[4])
    return jnp.concatenate([values_half, flat_ghosts], axis=2)


def scatter_one(terms, index_rows):
    width = terms.shape[-1]
    empty = jnp.zeros((OWN, width), jnp.float32)
    return empty.at[index_rows.reshape(-1)].add(terms.reshape(-1, width))


def owner_sum(local_terms, send_rows, live_mask):
    width = local_terms.shape[-1]
    rim_half = local_terms[:, :, OWN:].astype(jnp.bfloat16).reshape(N_ROW, N_COL, 4, TILE, width)
    returned = ghost_trade(rim_half)
    weighted = returned.astype(jnp.float32) * live_mask[..., None]
    summed = jax.vmap(jax.vmap(scatter_one))(weighted, send_rows)
    return local_terms[:, :, :OWN] + summed


def device_dot(left, right):
    flat_left = left.reshape((-1,) + left.shape[2:])
    flat_right = right.reshape((-1,) + right.shape[2:])
    products = lax.map(lambda pair: jnp.dot(pair[0], pair[1], preferred_element_type=jnp.float32), (flat_left, flat_right))
    return products.reshape(left.shape[:2] + products.shape[1:])


def reference(right_side, local_operator, local_inverse, coarse_basis, coarse_inverse, send_rows, send_count):
    positions = jnp.arange(TILE, dtype=jnp.int32)
    live_mask = (positions[None, None, None, :] < send_count[..., None]).astype(jnp.float32)
    inverse_whole = coarse_inverse.reshape(COARSE_ALL, COARSE_ALL)
    basis_turned = jnp.swapaxes(coarse_basis, 2, 3)
    solution = jnp.zeros(right_side.shape, jnp.float32)
    for sweep in range(ITERS):
        solution_half = solution.astype(jnp.bfloat16)
        image = owner_sum(device_dot(local_operator, with_ghosts(solution_half, send_rows, live_mask)), send_rows, live_mask)
        residual_half = (right_side - image).astype(jnp.bfloat16)
        residual_local = with_ghosts(residual_half, send_rows, live_mask)
        local_part = device_dot(local_inverse, residual_local)
        restricted = device_dot(basis_turned, residual_local).astype(jnp.bfloat16)
        coarse_level = jnp.dot(inverse_whole, restricted.reshape(COARSE_ALL, -1), preferred_element_type=jnp.float32).astype(jnp.bfloat16)
        coarse_level = coarse_level.reshape(N_ROW, N_COL, COARSE, -1)
        update = owner_sum(local_part + device_dot(coarse_basis, coarse_level), send_rows, live_mask)
        solution = solution + DAMPING * update
    return solution
```

```python
import functools

import jax
import jax.numpy as jnp
from jax import lax
from jax.experimental import pallas as pl
from jax.experimental.pallas import tpu as pltpu
from jax.sharding import PartitionSpec as P

ITERS = 3
DAMPING = 0.5
MESH = pl.DeviceIdType.MESH
OPPOSITE = (1, 0, 3, 2)
F32 = jnp.float32
HALF = jnp.bfloat16


def dot(left, right):
    return jnp.dot(left, right, preferred_element_type=F32)


def kernel(
    n_row, n_col,
    target_hbm, operator_hbm, inverse_hbm, basis_ref, coarse_hbm, rows_ref, counts_ref,
    out_ref,
    operator, inverse, coarse, target, basis_turned, pick, spread, total, values, held,
    packed, ghosts, gather_src, gathered, part_src, parts,
    load_sem, pack_send, pack_recv, gather_send, gather_recv, part_send, part_recv,
):
    own, width = target.shape
    tiles, tile = rows_ref.shape
    rim = tiles * tile
    level = basis_ref.shape[1]
    row = lax.axis_index("row")
    col = lax.axis_index("col")

    def at_row(step):
        return (lax.rem(row + step, n_row), col)

    def at_col(step):
        return (row, lax.rem(col + step, n_col))

    neighbours = (at_row(n_row - 1), at_row(1), at_col(n_col - 1), at_col(1))

    loads = [
        pltpu.make_async_copy(source, place, load_sem.at[i])
        for i, (source, place) in enumerate(
            (
                (target_hbm, target),
                (inverse_hbm, inverse),
                (coarse_hbm, coarse),
                (operator_hbm, operator),
            )
        )
    ]
    for load in loads:
        load.start()

    barrier = pltpu.get_barrier_semaphore()

    def greet_row(i, carry):
        pl.semaphore_signal(barrier, inc=1, device_id=at_row(i + 1), device_id_type=MESH)
        return carry

    def greet_col(i, carry):
        pl.semaphore_signal(barrier, inc=1, device_id=at_col(i + 1), device_id_type=MESH)
        return carry

    lax.fori_loop(0, n_row - 1, greet_row, 0)
    lax.fori_loop(0, n_col - 1, greet_col, 0)

    place = lax.broadcasted_iota(jnp.int32, (1, tile), 1)
    square = lax.broadcasted_iota(jnp.int32, (tile, tile), 0) == lax.broadcasted_iota(
        jnp.int32, (tile, tile), 1
    )
    for d in range(tiles):
        listed = jnp.where(place < counts_ref[0, d], rows_ref[d : d + 1, :], -1).astype(F32)
        down = lax.broadcasted_iota(jnp.int32, (own, tile), 0).astype(F32)
        spread[:, d * tile : (d + 1) * tile] = jnp.where(down == listed, 1.0, 0.0).astype(HALF)
        upright = jnp.sum(
            jnp.where(square, jnp.broadcast_to(listed, (tile, tile)), 0.0), axis=1, keepdims=True
        )
        along = lax.broadcasted_iota(jnp.int32, (tile, own), 1).astype(F32)
        pick[d * tile : (d + 1) * tile, :] = jnp.where(along == upright, 1.0, 0.0).astype(HALF)
    basis_turned[...] = basis_ref[...].astype(F32).T.astype(HALF)
    values[...] = jnp.zeros_like(values)

    pl.semaphore_wait(barrier, n_row + n_col - 2)

    def tile_copy(kind, sweep, d):
        return pltpu.make_async_remote_copy(
            src_ref=packed.at[kind, sweep, d],
            dst_ref=ghosts.at[kind, sweep, OPPOSITE[d]],
            send_sem=pack_send.at[kind, sweep, d],
            recv_sem=pack_recv.at[kind, sweep, OPPOSITE[d]],
            device_id=neighbours[d],
            device_id_type=MESH,
        )

    def send_tiles(kind, sweep, value):
        packed[kind, sweep] = value.astype(HALF).reshape(tiles, tile, width)
        for d in range(tiles):
            tile_copy(kind, sweep, d).start()

    def take_tiles(kind, sweep):
        for d in range(tiles):
            tile_copy(kind, sweep, d).wait_recv()
        return ghosts[kind, sweep].reshape(rim, width)

    def block_copy(sweep, step):
        return pltpu.make_async_remote_copy(
            src_ref=gather_src.at[sweep],
            dst_ref=gathered.at[sweep, col],
            send_sem=gather_send.at[sweep, step],
            recv_sem=gather_recv.at[sweep, step],
            device_id=at_col(step),
            device_id_type=MESH,
        )

    def part_copy(sweep, step):
        return pltpu.make_async_remote_copy(
            src_ref=part_src.at[sweep, lax.rem(row + step, n_row)],
            dst_ref=parts.at[sweep, row],
            send_sem=part_send.at[sweep, step],
            recv_sem=part_recv.at[sweep, step],
            device_id=at_row(step),
            device_id_type=MESH,
        )

    def every(count, act):
        def body(i, carry):
            act(i + 1)
            return carry

        lax.fori_loop(0, count - 1, body, 0)

    def sweep_once(sweep, carry):
        @pl.when(sweep == 0)
        def _():
            loads[0].wait()
            held[...] = target[...].astype(HALF)

        @pl.when(sweep > 0)
        def _():
            @pl.when(sweep == 1)
            def _():
                loads[3].wait()

            held[...] = values[...].astype(HALF)
            send_tiles(0, sweep, dot(pick[...], held[...]))
            total[...] = dot(operator[:, :own], held[...])
            margin = take_tiles(0, sweep)
            send_tiles(1, sweep, total[own:, :] + dot(operator[own:, own:], margin))
            total[:own, :] += dot(operator[:own, own:], margin)
            image = total[:own, :] + dot(spread[...], take_tiles(1, sweep))
            held[...] = (target[...] - image).astype(HALF)

        send_tiles(2, sweep, dot(pick[...], held[...]))

        @pl.when(sweep == 0)
        def _():
            loads[1].wait()
            loads[2].wait()

        total[...] = dot(inverse[:, :own], held[...])
        coarse_own = dot(basis_turned[:, :own], held[...])
        margin = take_tiles(2, sweep)
        restricted = (coarse_own + dot(basis_turned[:, own:], margin)).astype(HALF)
        gather_src[sweep] = restricted
        gathered[sweep, col] = restricted
        every(n_col, lambda step: block_copy(sweep, step).start())
        total[...] += dot(inverse[:, own:], margin)
        every(n_col, lambda step: block_copy(sweep, step).wait_recv())
        part = dot(coarse[...], gathered[sweep].reshape(n_col * level, width)).astype(HALF)
        part_src[sweep] = part.reshape(n_row, level, width)
        parts[sweep, row] = part_src[sweep, row]
        every(n_row, lambda step: part_copy(sweep, step).start())
        every(n_row, lambda step: part_copy(sweep, step).wait_recv())
        solved = jnp.sum(parts[sweep].astype(F32), axis=0).astype(HALF)
        send_tiles(3, sweep, total[own:, :] + dot(basis_ref[own:, :], solved))
        total[:own, :] += dot(basis_ref[:own, :], solved)
        values[...] += DAMPING * (total[:own, :] + dot(spread[...], take_tiles(3, sweep)))
        return carry

    lax.fori_loop(0, ITERS, sweep_once, 0)
    out_ref[...] = values[...]

    def settle(sweep, carry):
        @pl.when(sweep > 0)
        def _():
            for d in range(tiles):
                tile_copy(0, sweep, d).wait_send()
                tile_copy(1, sweep, d).wait_send()

        for d in range(tiles):
            tile_copy(2, sweep, d).wait_send()
            tile_copy(3, sweep, d).wait_send()
        every(n_col, lambda step: block_copy(sweep, step).wait_send())
        every(n_row, lambda step: part_copy(sweep, step).wait_send())
        return carry

    lax.fori_loop(0, ITERS, settle, 0)


def solution(mesh):
    n_row, n_col = mesh.shape["row"], mesh.shape["col"]

    def per_device(
        right_side, local_operator, local_inverse, coarse_basis, coarse_inverse, send_rows, send_count
    ):
        target = right_side[0, 0]
        own, width = target.shape
        basis = coarse_basis[0, 0]
        local, level = basis.shape
        rows_list = send_rows[0, 0]
        tiles, tile = rows_list.shape
        rim = tiles * tile
        turn = coarse_inverse.shape[2]
        coarse = coarse_inverse.reshape(-1, turn)
        vmem = pl.BlockSpec(memory_space=pltpu.VMEM)
        anywhere = pl.BlockSpec(memory_space=pl.ANY)
        out = pl.pallas_call(
            functools.partial(kernel, n_row, n_col),
            out_shape=jax.ShapeDtypeStruct((own, width), F32),
            in_specs=[
                anywhere, anywhere, anywhere, vmem, anywhere, vmem,
                pl.BlockSpec(memory_space=pltpu.SMEM),
            ],
            out_specs=vmem,
            scratch_shapes=[
                pltpu.VMEM((local, local), HALF),
                pltpu.VMEM((local, local), HALF),
                pltpu.VMEM(coarse.shape, HALF),
                pltpu.VMEM((own, width), F32),
                pltpu.VMEM((level, local), HALF),
                pltpu.VMEM((rim, own), HALF),
                pltpu.VMEM((own, rim), HALF),
                pltpu.VMEM((local, width), F32),
                pltpu.VMEM((own, width), F32),
                pltpu.VMEM((own, width), HALF),
                pltpu.VMEM((4, ITERS, tiles, tile, width), HALF),
                pltpu.VMEM((4, ITERS, tiles, tile, width), HALF),
                pltpu.VMEM((ITERS, level, width), HALF),
                pltpu.VMEM((ITERS, n_col, level, width), HALF),
                pltpu.VMEM((ITERS, n_row, level, width), HALF),
                pltpu.VMEM((ITERS, n_row, level, width), HALF),
                pltpu.SemaphoreType.DMA((4,)),
                pltpu.SemaphoreType.DMA((4, ITERS, tiles)),
                pltpu.SemaphoreType.DMA((4, ITERS, tiles)),
                pltpu.SemaphoreType.DMA((ITERS, n_col)),
                pltpu.SemaphoreType.DMA((ITERS, n_col)),
                pltpu.SemaphoreType.DMA((ITERS, n_row)),
                pltpu.SemaphoreType.DMA((ITERS, n_row)),
            ],
            compiler_params=pltpu.CompilerParams(
                collective_id=0, has_side_effects=True, vmem_limit_bytes=60 * 1024 * 1024
            ),
        )(
            target,
            local_operator[0, 0],
            local_inverse[0, 0],
            basis,
            coarse,
            rows_list,
            send_count[0],
        )
        return out[None, None]

    return jax.shard_map(
        per_device,
        mesh=mesh,
        in_specs=(
            P("row", "col", None, None),
            P("row", "col", None, None),
            P("row", "col", None, None),
            P("row", "col", None, None),
            P(None, "col", "row"),
            P("row", "col", None, None),
            P("row", "col", None),
        ),
        out_specs=P("row", "col", None, None),
        check_vma=False,
    )
```

```python
import functools

import jax
import jax.numpy as jnp
from jax import lax
from jax.experimental import pallas as pl
from jax.experimental.pallas import tpu as pltpu
from jax.sharding import PartitionSpec as P

ITERS = 3
DAMPING = 0.5
MESH = pl.DeviceIdType.MESH
OPPOSITE = (1, 0, 3, 2)
F32 = jnp.float32
HALF = jnp.bfloat16
STENCIL = (
    (0, 0), (-1, 0), (1, 0), (0, -1), (0, 1),
    (-2, 0), (2, 0), (-1, -1), (-1, 1), (1, -1), (1, 1), (0, -2), (0, 2),
)
NEAR = 5
OUTER_FIRST = tuple(range(NEAR, len(STENCIL))) + tuple(range(1, NEAR))


def stencil_index(down, right):
    return STENCIL.index((down, right))


def mirrored(k):
    return stencil_index(-STENCIL[k][0], -STENCIL[k][1])


def dot(left, right):
    return jnp.dot(left, right, preferred_element_type=F32)


def dot_turned(left, right):
    return lax.dot_general(left, right, (((1,), (1,)), ((), ())), preferred_element_type=F32)


def ring_steps(n_row, n_col):
    fast = 4
    half = n_col // 2
    rows = [(a, b) for a in range(n_row // fast) for b in range(fast)][1:]

    def row_hops(o):
        return 2 * min(o[0], n_row // fast - o[0]) + min(o[1], fast - o[1])

    cols = [(a, b, c) for a in range(2) for b in range(half // 2) for c in range(2)][1:]

    def col_hops(o):
        return o[0] + min(o[1], half // 2 - o[1])

    return sorted(rows, key=row_hops, reverse=True), sorted(cols, key=col_hops, reverse=True)


def kernel(
    n_row, n_col,
    target_hbm, operator_hbm, inverse_hbm, basis_ref, coarse_hbm, rows_ref, counts_ref,
    out_ref,
    operator, inverse, coarse, target, pick, spread, total, image, image_half, values, held, first,
    packed, ghosts, gather_src, gathered, part_src, parts, sums_src, sums, levels,
    basis_src, basis_tiles, wide_src, wide_tiles, assembled, psi, near_image, far_image,
    load_sem, pack_send, pack_recv, gather_send, gather_recv, part_send, part_recv,
    sums_send, sums_recv, level_send, level_recv, setup_send, setup_recv,
):
    own, width = target.shape
    tiles, tile = rows_ref.shape
    rim = tiles * tile
    level = basis_ref.shape[0]
    near = NEAR * level
    row = lax.axis_index("row")
    col = lax.axis_index("col")
    row_steps, col_steps = ring_steps(n_row, n_col)

    def at(down, right):
        return (
            lax.rem(row + (down + n_row), n_row) if down else row,
            lax.rem(col + (right + n_col), n_col) if right else col,
        )

    def row_peer(step):
        a, b = step
        return lax.rem(lax.div(row, 4) + a, n_row // 4) * 4 + lax.rem(lax.rem(row, 4) + b, 4)

    def col_peer(step):
        a, b, c = step
        quarter = n_col // 4
        return (
            lax.rem(lax.div(col, n_col // 2) + a, 2) * (n_col // 2)
            + lax.rem(lax.rem(lax.div(col, 2), quarter) + b, quarter) * 2
            + lax.rem(lax.rem(col, 2) + c, 2)
        )

    neighbours = [at(*STENCIL[1 + d]) for d in range(tiles)]

    loads = [
        pltpu.make_async_copy(source, place, load_sem.at[i])
        for i, (source, place) in enumerate(
            (
                (target_hbm, target),
                (inverse_hbm, inverse),
                (coarse_hbm, coarse),
                (operator_hbm, operator),
            )
        )
    ]
    for load in loads:
        load.start()

    barrier = pltpu.get_barrier_semaphore()
    greeted = 0
    for step in row_steps:
        pl.semaphore_signal(barrier, inc=1, device_id=(row_peer(step), col), device_id_type=MESH)
        greeted += 1
    for step in col_steps:
        pl.semaphore_signal(barrier, inc=1, device_id=(row, col_peer(step)), device_id_type=MESH)
        greeted += 1
    for down, right in STENCIL:
        if down and right:
            pl.semaphore_signal(barrier, inc=1, device_id=at(down, right), device_id_type=MESH)
            greeted += 1

    def tile_copy(kind, sweep, d):
        return pltpu.make_async_remote_copy(
            src_ref=packed.at[kind, sweep, d],
            dst_ref=ghosts.at[kind, sweep, OPPOSITE[d]],
            send_sem=pack_send.at[kind, sweep, d],
            recv_sem=pack_recv.at[kind, sweep, OPPOSITE[d]],
            device_id=neighbours[d],
            device_id_type=MESH,
        )

    def store_tiles(kind, sweep, value):
        packed[kind, sweep] = value.astype(HALF).reshape(tiles, tile, width)

    def start_tiles(kind, sweep):
        for d in range(tiles):
            tile_copy(kind, sweep, d).start()

    def send_tiles(kind, sweep, value):
        store_tiles(kind, sweep, value)
        start_tiles(kind, sweep)

    def take_tiles(kind, sweep):
        for d in range(tiles):
            tile_copy(kind, sweep, d).wait_recv()
        return ghosts[kind, sweep].reshape(rim, width)

    def setup_copy(stage, source, place, d):
        return pltpu.make_async_remote_copy(
            src_ref=source.at[d],
            dst_ref=place.at[OPPOSITE[d]],
            send_sem=setup_send.at[stage, d],
            recv_sem=setup_recv.at[stage, OPPOSITE[d]],
            device_id=neighbours[d],
            device_id_type=MESH,
        )

    def basis_copy(d):
        return setup_copy(0, basis_src, basis_tiles, d)

    def wide_copy(d):
        return setup_copy(1, wide_src, wide_tiles, d)

    def block_copy(sweep, i):
        return pltpu.make_async_remote_copy(
            src_ref=gather_src.at[sweep],
            dst_ref=gathered.at[sweep, col],
            send_sem=gather_send.at[sweep, i],
            recv_sem=gather_recv.at[sweep, i],
            device_id=(row, col_peer(col_steps[i])),
            device_id_type=MESH,
        )

    def part_copy(sweep, i):
        peer = row_peer(row_steps[i])
        return pltpu.make_async_remote_copy(
            src_ref=part_src.at[sweep, peer],
            dst_ref=parts.at[sweep, row],
            send_sem=part_send.at[sweep, i],
            recv_sem=part_recv.at[sweep, i],
            device_id=(peer, col),
            device_id_type=MESH,
        )

    def sum_copy(sweep, k):
        return pltpu.make_async_remote_copy(
            src_ref=sums_src.at[sweep, k],
            dst_ref=sums.at[sweep, mirrored(k)],
            send_sem=sums_send.at[sweep, k],
            recv_sem=sums_recv.at[sweep, mirrored(k)],
            device_id=at(*STENCIL[k]),
            device_id_type=MESH,
        )

    def level_copy(sweep, k):
        return pltpu.make_async_remote_copy(
            src_ref=levels.at[sweep, 0],
            dst_ref=levels.at[sweep, mirrored(k)],
            send_sem=level_send.at[sweep, k],
            recv_sem=level_recv.at[sweep, mirrored(k)],
            device_id=at(*STENCIL[k]),
            device_id_type=MESH,
        )

    def send_restricted(sweep, value):
        restricted = value.astype(HALF)
        gather_src[sweep] = restricted
        gathered[sweep, col] = restricted
        for i in range(n_col - 1):
            block_copy(sweep, i).start()

    def solve_part(sweep):
        for i in range(n_col - 1):
            block_copy(sweep, i).wait_recv()
        part = dot(coarse[...], gathered[sweep].reshape(n_col * level, width)).astype(HALF)
        part_src[sweep] = part.reshape(n_row, level, width)
        for i in range(n_row - 1):
            part_copy(sweep, i).start()
        parts[sweep, row] = part_src[sweep, row]

    def solve_rest(sweep, far):
        for i in range(n_row - 1):
            part_copy(sweep, i).wait_recv()
        levels[sweep, 0] = jnp.sum(parts[sweep].astype(F32), axis=0).astype(HALF)

        def outer():
            for k in range(NEAR, len(STENCIL)):
                level_copy(sweep, k).start()

        if far is True:
            outer()
        else:
            pl.when(far)(outer)
        for k in range(1, NEAR):
            level_copy(sweep, k).start()

    place = lax.broadcasted_iota(jnp.int32, (1, tile), 1)
    square = lax.broadcasted_iota(jnp.int32, (tile, tile), 0) == lax.broadcasted_iota(
        jnp.int32, (tile, tile), 1
    )
    lists = [
        jnp.where(place < counts_ref[0, d], rows_ref[d : d + 1, :], -1).astype(F32)
        for d in range(tiles)
    ]
    along = lax.broadcasted_iota(jnp.int32, (tile, own), 1).astype(F32)
    for d in range(tiles):
        upright = jnp.sum(
            jnp.where(square, jnp.broadcast_to(lists[d], (tile, tile)), 0.0), axis=1, keepdims=True
        )
        pick[d * tile : (d + 1) * tile, :] = jnp.where(along == upright, 1.0, 0.0).astype(HALF)
        basis_src[d] = basis_ref[:, own + d * tile : own + (d + 1) * tile]
    loads[0].wait()
    held[...] = target[...].astype(HALF)
    store_tiles(2, 0, dot(pick[...], held[...]))

    pl.semaphore_wait(barrier, greeted)

    start_tiles(2, 0)
    for d in range(tiles):
        basis_copy(d).start()
    down = lax.broadcasted_iota(jnp.int32, (own, tile), 0).astype(F32)
    for d in range(tiles):
        spread[:, d * tile : (d + 1) * tile] = jnp.where(down == lists[d], 1.0, 0.0).astype(HALF)
    assembled[...] = jnp.zeros_like(assembled)
    coarse_own = dot(basis_ref[:, :own], held[...])
    loads[1].wait()
    total[...] = dot(inverse[:, :own], held[...])
    margin = take_tiles(2, 0)
    first[...] = coarse_own + dot(basis_ref[:, own:], margin)
    send_restricted(0, first[...])
    total[...] += dot(inverse[:, own:], margin)
    send_tiles(3, 0, total[own:, :])

    assembled[:level, :own] = basis_ref[:, :own]
    for d in range(tiles):
        basis_copy(d).wait_recv()
    for d in range(tiles):
        assembled[(1 + d) * level : (2 + d) * level, :own] = dot(
            basis_tiles[d], pick[d * tile : (d + 1) * tile, :]
        ).astype(HALF)
    wide = dot(assembled[:near, :own], spread[...]).astype(HALF)
    for d in range(tiles):
        wide_src[d] = wide[:, d * tile : (d + 1) * tile]
    for d in range(tiles):
        wide_copy(d).start()

    loads[2].wait()
    solve_part(0)
    values[...] = DAMPING * (total[:own, :] + dot(spread[...], take_tiles(3, 0)))
    held[...] = values[...].astype(HALF)
    send_tiles(0, 0, dot(pick[...], held[...]))
    loads[3].wait()
    image[...] = dot(operator[:, :own], held[...])
    psi[...] = assembled[:near, :own].astype(F32).T.astype(HALF)
    for d in range(tiles):
        wide_copy(d).wait_recv()
    for d in range(tiles):
        for e in range(NEAR):
            k = stencil_index(
                STENCIL[1 + d][0] + STENCIL[e][0], STENCIL[1 + d][1] + STENCIL[e][1]
            )
            assembled[k * level : (k + 1) * level, own + d * tile : own + (d + 1) * tile] = (
                wide_tiles[d, e * level : (e + 1) * level, :]
            )
    near_image[...] = dot_turned(operator[...], assembled[:near, :]).astype(HALF)
    far_image[...] = dot_turned(operator[:, own:], assembled[near:, own:]).astype(HALF)
    image[...] += dot(operator[:, own:], take_tiles(0, 0))
    solve_rest(0, True)

    def take_near(sweep):
        for k in range(1, NEAR):
            level_copy(sweep, k).wait_recv()
        return levels[sweep, :NEAR].reshape(near, width)

    def sweep_once(sweep, carry):
        before = sweep - 1
        goes_on = sweep < ITERS - 1
        for k in range(NEAR, len(STENCIL)):
            level_copy(before, k).wait_recv()
        around = take_near(before)
        beyond = levels[before, NEAR:].reshape(-1, width)
        image[...] += DAMPING * (dot(near_image[...], around) + dot(far_image[...], beyond))
        image_half[...] = image[...].astype(HALF)
        near_sums = dot(assembled[:near, :], image_half[...])
        far_sums = dot(assembled[near:, own:], image_half[own:, :])
        sums_src[sweep, :NEAR] = near_sums.astype(HALF).reshape(NEAR, level, width)
        sums_src[sweep, NEAR:] = far_sums.astype(HALF).reshape(-1, level, width)
        for k in OUTER_FIRST:
            sum_copy(sweep, k).start()
        packed[1, sweep] = image_half[own:, :].reshape(tiles, tile, width)
        start_tiles(1, sweep)
        values[...] += DAMPING * dot(psi[...], around)

        for k in range(1, len(STENCIL)):
            sum_copy(sweep, k).wait_recv()
        sums[sweep, 0] = sums_src[sweep, 0]
        send_restricted(sweep, first[...] - jnp.sum(sums[sweep].astype(F32), axis=0))
        returned = take_tiles(1, sweep)
        held[...] = (target[...] - image[:own, :] - dot(spread[...], returned)).astype(HALF)
        send_tiles(2, sweep, dot(pick[...], held[...]))
        total[...] = dot(inverse[:, :own], held[...])
        solve_part(sweep)
        total[...] += dot(inverse[:, own:], take_tiles(2, sweep))
        send_tiles(3, sweep, total[own:, :])
        values[...] += DAMPING * (total[:own, :] + dot(spread[...], take_tiles(3, sweep)))

        @pl.when(goes_on)
        def _():
            held[...] = values[...].astype(HALF)
            send_tiles(0, sweep, dot(pick[...], held[...]))

        solve_rest(sweep, goes_on)

        @pl.when(goes_on)
        def _():
            image[...] = dot(operator[:, :own], held[...])
            image[...] += dot(operator[:, own:], take_tiles(0, sweep))

        return carry

    lax.fori_loop(1, ITERS, sweep_once, 0)
    out_ref[...] = values[...] + DAMPING * dot(psi[...], take_near(ITERS - 1))

    for d in range(tiles):
        basis_copy(d).wait_send()
        wide_copy(d).wait_send()

    def settle(sweep, carry):
        for d in range(tiles):
            tile_copy(2, sweep, d).wait_send()
            tile_copy(3, sweep, d).wait_send()
        for i in range(n_col - 1):
            block_copy(sweep, i).wait_send()
        for i in range(n_row - 1):
            part_copy(sweep, i).wait_send()
        for k in range(1, NEAR):
            level_copy(sweep, k).wait_send()

        @pl.when(sweep > 0)
        def _():
            for d in range(tiles):
                tile_copy(1, sweep, d).wait_send()
            for k in range(1, len(STENCIL)):
                sum_copy(sweep, k).wait_send()

        @pl.when(sweep < ITERS - 1)
        def _():
            for d in range(tiles):
                tile_copy(0, sweep, d).wait_send()
            for k in range(NEAR, len(STENCIL)):
                level_copy(sweep, k).wait_send()

        return carry

    lax.fori_loop(0, ITERS, settle, 0)


def solution(mesh):
    n_row, n_col = mesh.shape["row"], mesh.shape["col"]

    def per_device(
        right_side, local_operator, local_inverse, coarse_basis, coarse_inverse, send_rows, send_count
    ):
        target = right_side[0, 0]
        own, width = target.shape
        basis = coarse_basis[0, 0].T
        level, local = basis.shape
        rows_list = send_rows[0, 0]
        tiles, tile = rows_list.shape
        rim = tiles * tile
        coarse = coarse_inverse.reshape(-1, coarse_inverse.shape[2])
        points = len(STENCIL)
        near, far = NEAR * level, (points - NEAR) * level
        vmem = pl.BlockSpec(memory_space=pltpu.VMEM)
        anywhere = pl.BlockSpec(memory_space=pl.ANY)
        dma = pltpu.SemaphoreType.DMA
        out = pl.pallas_call(
            functools.partial(kernel, n_row, n_col),
            out_shape=jax.ShapeDtypeStruct((own, width), F32),
            in_specs=[
                anywhere, anywhere, anywhere, vmem, anywhere, vmem,
                pl.BlockSpec(memory_space=pltpu.SMEM),
            ],
            out_specs=vmem,
            scratch_shapes=[
                pltpu.VMEM((local, local), HALF),
                pltpu.VMEM((local, local), HALF),
                pltpu.VMEM(coarse.shape, HALF),
                pltpu.VMEM((own, width), F32),
                pltpu.VMEM((rim, own), HALF),
                pltpu.VMEM((own, rim), HALF),
                pltpu.VMEM((local, width), F32),
                pltpu.VMEM((local, width), F32),
                pltpu.VMEM((local, width), HALF),
                pltpu.VMEM((own, width), F32),
                pltpu.VMEM((own, width), HALF),
                pltpu.VMEM((level, width), F32),
                pltpu.VMEM((4, ITERS, tiles, tile, width), HALF),
                pltpu.VMEM((4, ITERS, tiles, tile, width), HALF),
                pltpu.VMEM((ITERS, level, width), HALF),
                pltpu.VMEM((ITERS, n_col, level, width), HALF),
                pltpu.VMEM((ITERS, n_row, level, width), HALF),
                pltpu.VMEM((ITERS, n_row, level, width), HALF),
                pltpu.VMEM((ITERS, points, level, width), HALF),
                pltpu.VMEM((ITERS, points, level, width), HALF),
                pltpu.VMEM((ITERS, points, level, width), HALF),
                pltpu.VMEM((tiles, level, tile), HALF),
                pltpu.VMEM((tiles, level, tile), HALF),
                pltpu.VMEM((tiles, near, tile), HALF),
                pltpu.VMEM((tiles, near, tile), HALF),
                pltpu.VMEM((near + far, local), HALF),
                pltpu.VMEM((own, near), HALF),
                pltpu.VMEM((local, near), HALF),
                pltpu.VMEM((local, far), HALF),
                dma((4,)),
                dma((4, ITERS, tiles)),
                dma((4, ITERS, tiles)),
                dma((ITERS, n_col - 1)),
                dma((ITERS, n_col - 1)),
                dma((ITERS, n_row - 1)),
                dma((ITERS, n_row - 1)),
                dma((ITERS, points)),
                dma((ITERS, points)),
                dma((ITERS, points)),
                dma((ITERS, points)),
                dma((2, tiles)),
                dma((2, tiles)),
            ],
            compiler_params=pltpu.CompilerParams(
                collective_id=0, has_side_effects=True, vmem_limit_bytes=60 * 1024 * 1024
            ),
        )(
            target,
            local_operator[0, 0],
            local_inverse[0, 0],
            basis,
            coarse,
            rows_list,
            send_count[0],
        )
        return out[None, None]

    return jax.shard_map(
        per_device,
        mesh=mesh,
        in_specs=(
            P("row", "col", None, None),
            P("row", "col", None, None),
            P("row", "col", None, None),
            P("row", "col", None, None),
            P(None, "col", "row"),
            P("row", "col", None, None),
            P("row", "col", None),
        ),
        out_specs=P("row", "col", None, None),
        check_vma=False,
    )
```

```python
import functools

import jax
import jax.numpy as jnp
from jax import lax
from jax.experimental import pallas as pl
from jax.experimental.pallas import tpu as pltpu
from jax.sharding import PartitionSpec as P

ITERS = 3
DAMPING = 0.5
MESH = pl.DeviceIdType.MESH
OPPOSITE = (1, 0, 3, 2)
F32 = jnp.float32
HALF = jnp.bfloat16
STENCIL = (
    (0, 0), (-1, 0), (1, 0), (0, -1), (0, 1),
    (-2, 0), (2, 0), (-1, -1), (-1, 1), (1, -1), (1, 1), (0, -2), (0, 2),
)
NEAR = 5
OUTER_FIRST = tuple(range(NEAR, len(STENCIL))) + tuple(range(1, NEAR))


def stencil_index(down, right):
    return STENCIL.index((down, right))


def mirrored(k):
    return stencil_index(-STENCIL[k][0], -STENCIL[k][1])


def dot(left, right):
    return jnp.dot(left, right, preferred_element_type=F32)


def dot_turned(left, right):
    return lax.dot_general(left, right, (((1,), (1,)), ((), ())), preferred_element_type=F32)


def ring_steps(n_row, n_col):
    fast = 4
    half = n_col // 2
    rows = [(a, b) for a in range(n_row // fast) for b in range(fast)][1:]

    def row_hops(o):
        return 2 * min(o[0], n_row // fast - o[0]) + min(o[1], fast - o[1])

    cols = [(a, b, c) for a in range(2) for b in range(half // 2) for c in range(2)][1:]

    def col_hops(o):
        return o[0] + min(o[1], half // 2 - o[1])

    return sorted(rows, key=row_hops, reverse=True), sorted(cols, key=col_hops, reverse=True)


def kernel(
    n_row, n_col,
    target_hbm, operator_hbm, inverse_hbm, basis_ref, coarse_hbm, rows_ref, counts_ref,
    values_out, psi_out, around_ref,
    operator, inverse, coarse, target, pick, spread, cross, ahead, total, image, values, held, first,
    packed, ghosts, gather_src, gathered, part_src, parts, sums_src, sums, levels,
    basis_src, basis_tiles, wide_src, wide_tiles, assembled, psi, near_image, far_image,
    ghost_sums, near_sums, far_sums, own_sums,
    load_sem, store_sem, pack_send, pack_recv, gather_send, gather_recv, part_send, part_recv,
    sums_send, sums_recv, level_send, level_recv, setup_send, setup_recv,
):
    own, width = target.shape
    tiles, tile = rows_ref.shape
    rim = tiles * tile
    level = basis_ref.shape[0]
    near = NEAR * level
    row = lax.axis_index("row")
    col = lax.axis_index("col")
    row_steps, col_steps = ring_steps(n_row, n_col)

    def at(down, right):
        return (
            lax.rem(row + (down + n_row), n_row) if down else row,
            lax.rem(col + (right + n_col), n_col) if right else col,
        )

    def row_peer(step):
        a, b = step
        return lax.rem(lax.div(row, 4) + a, n_row // 4) * 4 + lax.rem(lax.rem(row, 4) + b, 4)

    def col_peer(step):
        a, b, c = step
        quarter = n_col // 4
        return (
            lax.rem(lax.div(col, n_col // 2) + a, 2) * (n_col // 2)
            + lax.rem(lax.rem(lax.div(col, 2), quarter) + b, quarter) * 2
            + lax.rem(lax.rem(col, 2) + c, 2)
        )

    neighbours = [at(*STENCIL[1 + d]) for d in range(tiles)]

    loads = [
        pltpu.make_async_copy(source, place, load_sem.at[i])
        for i, (source, place) in enumerate(
            (
                (target_hbm, target),
                (inverse_hbm, inverse),
                (coarse_hbm, coarse),
                (operator_hbm, operator),
            )
        )
    ]
    for load in loads:
        load.start()

    barrier = pltpu.get_barrier_semaphore()
    greeted = 0
    for step in row_steps:
        pl.semaphore_signal(barrier, inc=1, device_id=(row_peer(step), col), device_id_type=MESH)
        greeted += 1
    for step in col_steps:
        pl.semaphore_signal(barrier, inc=1, device_id=(row, col_peer(step)), device_id_type=MESH)
        greeted += 1
    for down, right in STENCIL:
        if down and right:
            pl.semaphore_signal(barrier, inc=1, device_id=at(down, right), device_id_type=MESH)
            greeted += 1

    def tile_copy(kind, sweep, d):
        return pltpu.make_async_remote_copy(
            src_ref=packed.at[kind, sweep, d],
            dst_ref=ghosts.at[kind, sweep, OPPOSITE[d]],
            send_sem=pack_send.at[kind, sweep, d],
            recv_sem=pack_recv.at[kind, sweep, OPPOSITE[d]],
            device_id=neighbours[d],
            device_id_type=MESH,
        )

    def store_tiles(kind, sweep, value):
        packed[kind, sweep] = value.astype(HALF).reshape(tiles, tile, width)

    def start_tiles(kind, sweep):
        for d in range(tiles):
            tile_copy(kind, sweep, d).start()

    def send_tiles(kind, sweep, value):
        store_tiles(kind, sweep, value)
        start_tiles(kind, sweep)

    def take_tiles(kind, sweep):
        for d in range(tiles):
            tile_copy(kind, sweep, d).wait_recv()
        return ghosts[kind, sweep].reshape(rim, width)

    def setup_copy(stage, source, place, d):
        return pltpu.make_async_remote_copy(
            src_ref=source.at[d],
            dst_ref=place.at[OPPOSITE[d]],
            send_sem=setup_send.at[stage, d],
            recv_sem=setup_recv.at[stage, OPPOSITE[d]],
            device_id=neighbours[d],
            device_id_type=MESH,
        )

    def basis_copy(d):
        return setup_copy(0, basis_src, basis_tiles, d)

    def wide_copy(d):
        return setup_copy(1, wide_src, wide_tiles, d)

    def block_copy(sweep, i):
        return pltpu.make_async_remote_copy(
            src_ref=gather_src.at[sweep],
            dst_ref=gathered.at[sweep, col],
            send_sem=gather_send.at[sweep, i],
            recv_sem=gather_recv.at[sweep, i],
            device_id=(row, col_peer(col_steps[i])),
            device_id_type=MESH,
        )

    def part_copy(sweep, i):
        peer = row_peer(row_steps[i])
        return pltpu.make_async_remote_copy(
            src_ref=part_src.at[sweep, peer],
            dst_ref=parts.at[sweep, row],
            send_sem=part_send.at[sweep, i],
            recv_sem=part_recv.at[sweep, i],
            device_id=(peer, col),
            device_id_type=MESH,
        )

    def sum_copy(sweep, k):
        return pltpu.make_async_remote_copy(
            src_ref=sums_src.at[sweep, k],
            dst_ref=sums.at[sweep, mirrored(k)],
            send_sem=sums_send.at[sweep, k],
            recv_sem=sums_recv.at[sweep, mirrored(k)],
            device_id=at(*STENCIL[k]),
            device_id_type=MESH,
        )

    def level_copy(sweep, k):
        return pltpu.make_async_remote_copy(
            src_ref=levels.at[sweep, 0],
            dst_ref=levels.at[sweep, mirrored(k)],
            send_sem=level_send.at[sweep, k],
            recv_sem=level_recv.at[sweep, mirrored(k)],
            device_id=at(*STENCIL[k]),
            device_id_type=MESH,
        )

    def send_restricted(sweep, value):
        restricted = value.astype(HALF)
        gather_src[sweep] = restricted
        gathered[sweep, col] = restricted
        for i in range(n_col - 1):
            block_copy(sweep, i).start()

    def solve_part(sweep):
        for i in range(n_col - 1):
            block_copy(sweep, i).wait_recv()
        part = dot(coarse[...], gathered[sweep].reshape(n_col * level, width)).astype(HALF)
        part_src[sweep] = part.reshape(n_row, level, width)
        for i in range(n_row - 1):
            part_copy(sweep, i).start()
        parts[sweep, row] = part_src[sweep, row]

    def solve_rest(sweep, far):
        for i in range(n_row - 1):
            part_copy(sweep, i).wait_recv()
        levels[sweep, 0] = jnp.sum(parts[sweep].astype(F32), axis=0).astype(HALF)

        def outer():
            for k in range(NEAR, len(STENCIL)):
                level_copy(sweep, k).start()

        if far is True:
            outer()
        else:
            pl.when(far)(outer)
        for k in range(1, NEAR):
            level_copy(sweep, k).start()

    def sums_of_own():
        own_sums[:near, :] = dot(assembled[:near, :], image[...].astype(HALF))
        own_sums[near:, :] = dot(assembled[near:, own:], image[own:, :].astype(HALF))

    def pick_ahead(value):
        coarser = value.astype(HALF)
        finer = (value - coarser.astype(F32)).astype(HALF)
        ahead[...] = dot(pick[...], coarser) + dot(pick[...], finer)

    place = lax.broadcasted_iota(jnp.int32, (1, tile), 1)
    square = lax.broadcasted_iota(jnp.int32, (tile, tile), 0) == lax.broadcasted_iota(
        jnp.int32, (tile, tile), 1
    )
    lists = [
        jnp.where(place < counts_ref[0, d], rows_ref[d : d + 1, :], -1).astype(F32)
        for d in range(tiles)
    ]
    along = lax.broadcasted_iota(jnp.int32, (tile, own), 1).astype(F32)
    for d in range(tiles):
        upright = jnp.sum(
            jnp.where(square, jnp.broadcast_to(lists[d], (tile, tile)), 0.0), axis=1, keepdims=True
        )
        pick[d * tile : (d + 1) * tile, :] = jnp.where(along == upright, 1.0, 0.0).astype(HALF)
        basis_src[d] = basis_ref[:, own + d * tile : own + (d + 1) * tile]
    loads[0].wait()
    held[...] = target[...].astype(HALF)
    store_tiles(2, 0, dot(pick[...], held[...]))

    pl.semaphore_wait(barrier, greeted)

    start_tiles(2, 0)
    for d in range(tiles):
        basis_copy(d).start()
    down = lax.broadcasted_iota(jnp.int32, (own, tile), 0).astype(F32)
    for d in range(tiles):
        spread[:, d * tile : (d + 1) * tile] = jnp.where(down == lists[d], 1.0, 0.0).astype(HALF)
    cross[...] = dot(pick[...], spread[...]).astype(HALF)
    assembled[...] = jnp.zeros_like(assembled)
    coarse_own = dot(basis_ref[:, :own], held[...])
    loads[1].wait()
    total[...] = dot(inverse[:, :own], held[...])
    margin = take_tiles(2, 0)
    first[...] = coarse_own + dot(basis_ref[:, own:], margin)
    send_restricted(0, first[...])
    send_tiles(3, 0, total[own:, :] + dot(inverse[own:, own:], margin))
    total[:own, :] += dot(inverse[:own, own:], margin)

    assembled[:level, :own] = basis_ref[:, :own]
    for d in range(tiles):
        basis_copy(d).wait_recv()
    for d in range(tiles):
        assembled[(1 + d) * level : (2 + d) * level, :own] = dot(
            basis_tiles[d], pick[d * tile : (d + 1) * tile, :]
        ).astype(HALF)
    wide = dot(assembled[:near, :own], spread[...]).astype(HALF)
    for d in range(tiles):
        wide_src[d] = wide[:, d * tile : (d + 1) * tile]
    for d in range(tiles):
        wide_copy(d).start()

    loads[2].wait()
    solve_part(0)
    values[...] = DAMPING * total[:own, :]
    pick_ahead(values[...])
    returned = take_tiles(3, 0)
    send_tiles(0, 0, ahead[...] + DAMPING * dot(cross[...], returned))
    values[...] += DAMPING * dot(spread[...], returned)
    held[...] = values[...].astype(HALF)
    loads[3].wait()
    image[...] = dot(operator[:, :own], held[...])
    psi[...] = assembled[:near, :own].astype(F32).T.astype(HALF)
    psi_store = pltpu.make_async_copy(psi, psi_out, store_sem.at[0])
    psi_store.start()
    for d in range(tiles):
        wide_copy(d).wait_recv()
    for d in range(tiles):
        for e in range(NEAR):
            k = stencil_index(
                STENCIL[1 + d][0] + STENCIL[e][0], STENCIL[1 + d][1] + STENCIL[e][1]
            )
            assembled[k * level : (k + 1) * level, own + d * tile : own + (d + 1) * tile] = (
                wide_tiles[d, e * level : (e + 1) * level, :]
            )
    near_image[...] = dot_turned(operator[...], assembled[:near, :]).astype(HALF)
    far_image[...] = dot_turned(operator[:, own:], assembled[near:, own:]).astype(HALF)
    solve_rest(0, True)
    ghost_sums[:near, :] = dot(assembled[:near, :], operator[:, own:]).astype(HALF)
    ghost_sums[near:, :] = dot(assembled[near:, own:], operator[own:, own:]).astype(HALF)
    near_sums[:near, :] = dot(assembled[:near, :], near_image[...]).astype(HALF)
    near_sums[near:, :] = dot(assembled[near:, own:], near_image[own:, :]).astype(HALF)
    far_sums[:near, :] = dot(assembled[:near, :], far_image[...]).astype(HALF)
    far_sums[near:, :] = dot(assembled[near:, own:], far_image[own:, :]).astype(HALF)
    sums_of_own()

    def values_store():
        return pltpu.make_async_copy(values, values_out, store_sem.at[1])

    def take_near(sweep):
        for k in range(1, NEAR):
            level_copy(sweep, k).wait_recv()
        return levels[sweep, :NEAR].reshape(near, width)

    def sweep_once(sweep, carry):
        before = sweep - 1
        goes_on = sweep < ITERS - 1
        margin = take_tiles(0, before)
        image[own:, :] += dot(operator[own:, own:], margin)
        own_sums[...] += dot(ghost_sums[...], margin)
        for k in range(NEAR, len(STENCIL)):
            level_copy(before, k).wait_recv()
        around = take_near(before)
        beyond = levels[before, NEAR:].reshape(-1, width)
        owed = own_sums[...] + DAMPING * (dot(near_sums[...], around) + dot(far_sums[...], beyond))
        sums_src[sweep] = owed.astype(HALF).reshape(len(STENCIL), level, width)
        for k in OUTER_FIRST:
            sum_copy(sweep, k).start()
        send_tiles(
            1,
            sweep,
            image[own:, :]
            + DAMPING * (dot(near_image[own:, :], around) + dot(far_image[own:, :], beyond)),
        )
        image[:own, :] += dot(operator[:own, own:], margin) + DAMPING * (
            dot(near_image[:own, :], around) + dot(far_image[:own, :], beyond)
        )
        total[:own, :] = target[...] - image[:own, :]
        pick_ahead(total[:own, :])
        values[...] += DAMPING * dot(psi[...], around)

        for k in range(1, len(STENCIL)):
            sum_copy(sweep, k).wait_recv()
        sums[sweep, 0] = sums_src[sweep, 0]
        send_restricted(sweep, first[...] - jnp.sum(sums[sweep].astype(F32), axis=0))
        returned = take_tiles(1, sweep)
        send_tiles(2, sweep, ahead[...] - dot(cross[...], returned))
        held[...] = (total[:own, :] - dot(spread[...], returned)).astype(HALF)
        total[...] = dot(inverse[:, :own], held[...])
        solve_part(sweep)
        arrived = take_tiles(2, sweep)
        send_tiles(3, sweep, total[own:, :] + dot(inverse[own:, own:], arrived))
        values[...] += DAMPING * (total[:own, :] + dot(inverse[:own, own:], arrived))

        @pl.when(goes_on)
        def _():
            pick_ahead(values[...])

        solve_rest(sweep, goes_on)

        returned = take_tiles(3, sweep)

        @pl.when(goes_on)
        def _():
            send_tiles(0, sweep, ahead[...] + DAMPING * dot(cross[...], returned))

        values[...] += DAMPING * dot(spread[...], returned)

        @pl.when(sweep == ITERS - 1)
        def _():
            values_store().start()

        @pl.when(goes_on)
        def _():
            image[...] = dot(operator[:, :own], values[...].astype(HALF))
            sums_of_own()

        return carry

    lax.fori_loop(1, ITERS, sweep_once, 0)
    around_ref[...] = take_near(ITERS - 1)
    psi_store.wait()
    values_store().wait()

    for d in range(tiles):
        basis_copy(d).wait_send()
        wide_copy(d).wait_send()

    def settle(sweep, carry):
        for d in range(tiles):
            tile_copy(2, sweep, d).wait_send()
            tile_copy(3, sweep, d).wait_send()
        for i in range(n_col - 1):
            block_copy(sweep, i).wait_send()
        for i in range(n_row - 1):
            part_copy(sweep, i).wait_send()
        for k in range(1, NEAR):
            level_copy(sweep, k).wait_send()

        @pl.when(sweep > 0)
        def _():
            for d in range(tiles):
                tile_copy(1, sweep, d).wait_send()
            for k in range(1, len(STENCIL)):
                sum_copy(sweep, k).wait_send()

        @pl.when(sweep < ITERS - 1)
        def _():
            for d in range(tiles):
                tile_copy(0, sweep, d).wait_send()
            for k in range(NEAR, len(STENCIL)):
                level_copy(sweep, k).wait_send()

        return carry

    lax.fori_loop(0, ITERS, settle, 0)


def solution(mesh):
    n_row, n_col = mesh.shape["row"], mesh.shape["col"]

    def per_device(
        right_side, local_operator, local_inverse, coarse_basis, coarse_inverse, send_rows, send_count
    ):
        target = right_side[0, 0]
        own, width = target.shape
        basis = coarse_basis[0, 0].T
        level, local = basis.shape
        rows_list = send_rows[0, 0]
        tiles, tile = rows_list.shape
        rim = tiles * tile
        coarse = coarse_inverse.reshape(-1, coarse_inverse.shape[2])
        points = len(STENCIL)
        near, far = NEAR * level, (points - NEAR) * level
        vmem = pl.BlockSpec(memory_space=pltpu.VMEM)
        anywhere = pl.BlockSpec(memory_space=pl.ANY)
        dma = pltpu.SemaphoreType.DMA
        values, psi, around = pl.pallas_call(
            functools.partial(kernel, n_row, n_col),
            out_shape=(
                jax.ShapeDtypeStruct((own, width), F32),
                jax.ShapeDtypeStruct((own, near), HALF),
                jax.ShapeDtypeStruct((near, width), HALF),
            ),
            in_specs=[
                anywhere, anywhere, anywhere, vmem, anywhere, vmem,
                pl.BlockSpec(memory_space=pltpu.SMEM),
            ],
            out_specs=(anywhere, anywhere, vmem),
            scratch_shapes=[
                pltpu.VMEM((local, local), HALF),
                pltpu.VMEM((local, local), HALF),
                pltpu.VMEM(coarse.shape, HALF),
                pltpu.VMEM((own, width), F32),
                pltpu.VMEM((rim, own), HALF),
                pltpu.VMEM((own, rim), HALF),
                pltpu.VMEM((rim, rim), HALF),
                pltpu.VMEM((rim, width), F32),
                pltpu.VMEM((local, width), F32),
                pltpu.VMEM((local, width), F32),
                pltpu.VMEM((own, width), F32),
                pltpu.VMEM((own, width), HALF),
                pltpu.VMEM((level, width), F32),
                pltpu.VMEM((4, ITERS, tiles, tile, width), HALF),
                pltpu.VMEM((4, ITERS, tiles, tile, width), HALF),
                pltpu.VMEM((ITERS, level, width), HALF),
                pltpu.VMEM((ITERS, n_col, level, width), HALF),
                pltpu.VMEM((ITERS, n_row, level, width), HALF),
                pltpu.VMEM((ITERS, n_row, level, width), HALF),
                pltpu.VMEM((ITERS, points, level, width), HALF),
                pltpu.VMEM((ITERS, points, level, width), HALF),
                pltpu.VMEM((ITERS, points, level, width), HALF),
                pltpu.VMEM((tiles, level, tile), HALF),
                pltpu.VMEM((tiles, level, tile), HALF),
                pltpu.VMEM((tiles, near, tile), HALF),
                pltpu.VMEM((tiles, near, tile), HALF),
                pltpu.VMEM((near + far, local), HALF),
                pltpu.VMEM((own, near), HALF),
                pltpu.VMEM((local, near), HALF),
                pltpu.VMEM((local, far), HALF),
                pltpu.VMEM((near + far, rim), HALF),
                pltpu.VMEM((near + far, near), HALF),
                pltpu.VMEM((near + far, far), HALF),
                pltpu.VMEM((near + far, width), F32),
                dma((4,)),
                dma((2,)),
                dma((4, ITERS, tiles)),
                dma((4, ITERS, tiles)),
                dma((ITERS, n_col - 1)),
                dma((ITERS, n_col - 1)),
                dma((ITERS, n_row - 1)),
                dma((ITERS, n_row - 1)),
                dma((ITERS, points)),
                dma((ITERS, points)),
                dma((ITERS, points)),
                dma((ITERS, points)),
                dma((2, tiles)),
                dma((2, tiles)),
            ],
            compiler_params=pltpu.CompilerParams(
                collective_id=0, has_side_effects=True, vmem_limit_bytes=60 * 1024 * 1024
            ),
        )(
            target,
            local_operator[0, 0],
            local_inverse[0, 0],
            basis,
            coarse,
            rows_list,
            send_count[0],
        )
        return (values + DAMPING * dot(psi, around))[None, None]

    return jax.shard_map(
        per_device,
        mesh=mesh,
        in_specs=(
            P("row", "col", None, None),
            P("row", "col", None, None),
            P("row", "col", None, None),
            P("row", "col", None, None),
            P(None, "col", "row"),
            P("row", "col", None, None),
            P("row", "col", None),
        ),
        out_specs=P("row", "col", None, None),
        check_vma=False,
    )
```

```python
import functools

import jax
import jax.numpy as jnp
from jax import lax
from jax.experimental import pallas as pl
from jax.experimental.pallas import tpu as pltpu
from jax.sharding import PartitionSpec as P

ITERS = 3
DAMPING = 0.5
MESH = pl.DeviceIdType.MESH
OPPOSITE = (1, 0, 3, 2)
F32 = jnp.float32
HALF = jnp.bfloat16
STENCIL = (
    (0, 0), (-1, 0), (1, 0), (0, -1), (0, 1),
    (-2, 0), (2, 0), (-1, -1), (-1, 1), (1, -1), (1, 1), (0, -2), (0, 2),
)
NEAR = 5
OUTER_FIRST = tuple(range(NEAR, len(STENCIL))) + tuple(range(1, NEAR))


def stencil_index(down, right):
    return STENCIL.index((down, right))


def mirrored(k):
    return stencil_index(-STENCIL[k][0], -STENCIL[k][1])


def dot(left, right):
    return jnp.dot(left, right, preferred_element_type=F32)


def dot_turned(left, right):
    return lax.dot_general(left, right, (((1,), (1,)), ((), ())), preferred_element_type=F32)


def ring_steps(n_row, n_col):
    fast = 4
    half = n_col // 2
    rows = [(a, b) for a in range(n_row // fast) for b in range(fast)][1:]

    def row_hops(o):
        return 2 * min(o[0], n_row // fast - o[0]) + min(o[1], fast - o[1])

    cols = [(a, b, c) for a in range(2) for b in range(half // 2) for c in range(2)][1:]

    def col_hops(o):
        return o[0] + min(o[1], half // 2 - o[1])

    return sorted(rows, key=row_hops, reverse=True), sorted(cols, key=col_hops, reverse=True)


def kernel(
    n_row, n_col,
    target_hbm, operator_hbm, inverse_hbm, basis_hbm, coarse_hbm, rows_hbm, counts_hbm,
    values_out, psi_out, around_ref,
    operator, inverse, coarse, target, basis_ref, rows_ref, counts_ref, pick, spread, cross, ahead, total, image, values, held, first,
    packed, ghosts, gather_src, gathered, part_src, parts, sums_src, sums, levels,
    basis_src, basis_tiles, wide_src, wide_tiles, assembled, psi, near_image, far_image,
    ghost_sums, near_sums, far_sums, own_sums,
    load_sem, store_sem, pack_send, pack_recv, gather_send, gather_recv, part_send, part_recv,
    sums_send, sums_recv, level_send, level_recv, setup_send, setup_recv,
):
    own, width = target.shape
    tiles, tile = rows_ref.shape
    rim = tiles * tile
    level = basis_ref.shape[0]
    near = NEAR * level
    row = lax.axis_index("row")
    col = lax.axis_index("col")
    row_steps, col_steps = ring_steps(n_row, n_col)

    def at(down, right):
        return (
            lax.rem(row + (down + n_row), n_row) if down else row,
            lax.rem(col + (right + n_col), n_col) if right else col,
        )

    def row_peer(step):
        a, b = step
        return lax.rem(lax.div(row, 4) + a, n_row // 4) * 4 + lax.rem(lax.rem(row, 4) + b, 4)

    def col_peer(step):
        a, b, c = step
        quarter = n_col // 4
        return (
            lax.rem(lax.div(col, n_col // 2) + a, 2) * (n_col // 2)
            + lax.rem(lax.rem(lax.div(col, 2), quarter) + b, quarter) * 2
            + lax.rem(lax.rem(col, 2) + c, 2)
        )

    neighbours = [at(*STENCIL[1 + d]) for d in range(tiles)]

    loads = [
        pltpu.make_async_copy(source, place, load_sem.at[i])
        for i, (source, place) in enumerate(
            (
                (target_hbm, target),
                (inverse_hbm, inverse),
                (coarse_hbm, coarse),
                (operator_hbm, operator),
                (rows_hbm, rows_ref),
                (counts_hbm, counts_ref),
                (basis_hbm, basis_ref),
            )
        )
    ]
    for i in (4, 5, 0, 6, 1, 2, 3):
        loads[i].start()

    barrier = pltpu.get_barrier_semaphore()
    greeted = 0
    for step in row_steps:
        pl.semaphore_signal(barrier, inc=1, device_id=(row_peer(step), col), device_id_type=MESH)
        greeted += 1
    for step in col_steps:
        pl.semaphore_signal(barrier, inc=1, device_id=(row, col_peer(step)), device_id_type=MESH)
        greeted += 1
    for down, right in STENCIL:
        if down and right:
            pl.semaphore_signal(barrier, inc=1, device_id=at(down, right), device_id_type=MESH)
            greeted += 1

    def tile_copy(kind, sweep, d):
        return pltpu.make_async_remote_copy(
            src_ref=packed.at[kind, sweep, d],
            dst_ref=ghosts.at[kind, sweep, OPPOSITE[d]],
            send_sem=pack_send.at[kind, sweep, d],
            recv_sem=pack_recv.at[kind, sweep, OPPOSITE[d]],
            device_id=neighbours[d],
            device_id_type=MESH,
        )

    def store_tiles(kind, sweep, value):
        packed[kind, sweep] = value.astype(HALF).reshape(tiles, tile, width)

    def start_tiles(kind, sweep):
        for d in range(tiles):
            tile_copy(kind, sweep, d).start()

    def send_tiles(kind, sweep, value):
        store_tiles(kind, sweep, value)
        start_tiles(kind, sweep)

    def take_tiles(kind, sweep):
        for d in range(tiles):
            tile_copy(kind, sweep, d).wait_recv()
        return ghosts[kind, sweep].reshape(rim, width)

    def setup_copy(stage, source, place, d):
        return pltpu.make_async_remote_copy(
            src_ref=source.at[d],
            dst_ref=place.at[OPPOSITE[d]],
            send_sem=setup_send.at[stage, d],
            recv_sem=setup_recv.at[stage, OPPOSITE[d]],
            device_id=neighbours[d],
            device_id_type=MESH,
        )

    def basis_copy(d):
        return setup_copy(0, basis_src, basis_tiles, d)

    def wide_copy(d):
        return setup_copy(1, wide_src, wide_tiles, d)

    def block_copy(sweep, i):
        return pltpu.make_async_remote_copy(
            src_ref=gather_src.at[sweep],
            dst_ref=gathered.at[sweep, col],
            send_sem=gather_send.at[sweep, i],
            recv_sem=gather_recv.at[sweep, i],
            device_id=(row, col_peer(col_steps[i])),
            device_id_type=MESH,
        )

    def part_copy(sweep, i):
        peer = row_peer(row_steps[i])
        return pltpu.make_async_remote_copy(
            src_ref=part_src.at[sweep, peer],
            dst_ref=parts.at[sweep, row],
            send_sem=part_send.at[sweep, i],
            recv_sem=part_recv.at[sweep, i],
            device_id=(peer, col),
            device_id_type=MESH,
        )

    def sum_copy(sweep, k):
        return pltpu.make_async_remote_copy(
            src_ref=sums_src.at[sweep, k],
            dst_ref=sums.at[sweep, mirrored(k)],
            send_sem=sums_send.at[sweep, k],
            recv_sem=sums_recv.at[sweep, mirrored(k)],
            device_id=at(*STENCIL[k]),
            device_id_type=MESH,
        )

    def level_copy(sweep, k):
        return pltpu.make_async_remote_copy(
            src_ref=levels.at[sweep, 0],
            dst_ref=levels.at[sweep, mirrored(k)],
            send_sem=level_send.at[sweep, k],
            recv_sem=level_recv.at[sweep, mirrored(k)],
            device_id=at(*STENCIL[k]),
            device_id_type=MESH,
        )

    def send_restricted(sweep, value):
        restricted = value.astype(HALF)
        gather_src[sweep] = restricted
        gathered[sweep, col] = restricted
        for i in range(n_col - 1):
            block_copy(sweep, i).start()

    def solve_part(sweep):
        for i in range(n_col - 1):
            block_copy(sweep, i).wait_recv()
        part = dot(coarse[...], gathered[sweep].reshape(n_col * level, width)).astype(HALF)
        part_src[sweep] = part.reshape(n_row, level, width)
        for i in range(n_row - 1):
            part_copy(sweep, i).start()
        parts[sweep, row] = part_src[sweep, row]

    def solve_rest(sweep, far):
        for i in range(n_row - 1):
            part_copy(sweep, i).wait_recv()
        levels[sweep, 0] = jnp.sum(parts[sweep].astype(F32), axis=0).astype(HALF)

        def outer():
            for k in range(NEAR, len(STENCIL)):
                level_copy(sweep, k).start()

        if far is True:
            outer()
        else:
            pl.when(far)(outer)
        for k in range(1, NEAR):
            level_copy(sweep, k).start()

    def sums_of_own():
        own_sums[:near, :] = dot(assembled[:near, :], image[...].astype(HALF))
        own_sums[near:, :] = dot(assembled[near:, own:], image[own:, :].astype(HALF))

    def pick_ahead(value):
        coarser = value.astype(HALF)
        finer = (value - coarser.astype(F32)).astype(HALF)
        ahead[...] = dot(pick[...], coarser) + dot(pick[...], finer)

    place = lax.broadcasted_iota(jnp.int32, (1, tile), 1)
    square = lax.broadcasted_iota(jnp.int32, (tile, tile), 0) == lax.broadcasted_iota(
        jnp.int32, (tile, tile), 1
    )
    loads[4].wait()
    loads[5].wait()
    lists = [
        jnp.where(place < counts_ref[:, d : d + 1], rows_ref[d : d + 1, :], -1).astype(F32)
        for d in range(tiles)
    ]
    along = lax.broadcasted_iota(jnp.int32, (tile, own), 1).astype(F32)
    for d in range(tiles):
        upright = jnp.sum(
            jnp.where(square, jnp.broadcast_to(lists[d], (tile, tile)), 0.0), axis=1, keepdims=True
        )
        pick[d * tile : (d + 1) * tile, :] = jnp.where(along == upright, 1.0, 0.0).astype(HALF)
    loads[6].wait()
    for d in range(tiles):
        basis_src[d] = basis_ref[:, own + d * tile : own + (d + 1) * tile]
    loads[0].wait()
    held[...] = target[...].astype(HALF)
    store_tiles(2, 0, dot(pick[...], held[...]))

    pl.semaphore_wait(barrier, greeted)

    start_tiles(2, 0)
    for d in range(tiles):
        basis_copy(d).start()
    down = lax.broadcasted_iota(jnp.int32, (own, tile), 0).astype(F32)
    for d in range(tiles):
        spread[:, d * tile : (d + 1) * tile] = jnp.where(down == lists[d], 1.0, 0.0).astype(HALF)
    cross[...] = dot(pick[...], spread[...]).astype(HALF)
    assembled[...] = jnp.zeros_like(assembled)
    coarse_own = dot(basis_ref[:, :own], held[...])
    loads[1].wait()
    total[...] = dot(inverse[:, :own], held[...])
    margin = take_tiles(2, 0)
    first[...] = coarse_own + dot(basis_ref[:, own:], margin)
    send_restricted(0, first[...])
    send_tiles(3, 0, total[own:, :] + dot(inverse[own:, own:], margin))
    total[:own, :] += dot(inverse[:own, own:], margin)

    assembled[:level, :own] = basis_ref[:, :own]
    for d in range(tiles):
        basis_copy(d).wait_recv()
    for d in range(tiles):
        assembled[(1 + d) * level : (2 + d) * level, :own] = dot(
            basis_tiles[d], pick[d * tile : (d + 1) * tile, :]
        ).astype(HALF)
    wide = dot(assembled[:near, :own], spread[...]).astype(HALF)
    for d in range(tiles):
        wide_src[d] = wide[:, d * tile : (d + 1) * tile]
    for d in range(tiles):
        wide_copy(d).start()

    loads[2].wait()
    solve_part(0)
    values[...] = DAMPING * total[:own, :]
    pick_ahead(values[...])
    returned = take_tiles(3, 0)
    send_tiles(0, 0, ahead[...] + DAMPING * dot(cross[...], returned))
    values[...] += DAMPING * dot(spread[...], returned)
    held[...] = values[...].astype(HALF)
    loads[3].wait()
    image[...] = dot(operator[:, :own], held[...])
    psi[...] = assembled[:near, :own].astype(F32).T.astype(HALF)
    psi_store = pltpu.make_async_copy(psi, psi_out, store_sem.at[0])
    psi_store.start()
    for d in range(tiles):
        wide_copy(d).wait_recv()
    for d in range(tiles):
        for e in range(NEAR):
            k = stencil_index(
                STENCIL[1 + d][0] + STENCIL[e][0], STENCIL[1 + d][1] + STENCIL[e][1]
            )
            assembled[k * level : (k + 1) * level, own + d * tile : own + (d + 1) * tile] = (
                wide_tiles[d, e * level : (e + 1) * level, :]
            )
    solve_rest(0, True)
    near_image[...] = dot_turned(operator[...], assembled[:near, :]).astype(HALF)
    far_image[...] = dot_turned(operator[:, own:], assembled[near:, own:]).astype(HALF)
    ghost_sums[:near, :] = dot(assembled[:near, :], operator[:, own:]).astype(HALF)
    ghost_sums[near:, :] = dot(assembled[near:, own:], operator[own:, own:]).astype(HALF)
    near_sums[:near, :] = dot(assembled[:near, :], near_image[...]).astype(HALF)
    near_sums[near:, :] = dot(assembled[near:, own:], near_image[own:, :]).astype(HALF)
    far_sums[:near, :] = dot(assembled[:near, :], far_image[...]).astype(HALF)
    far_sums[near:, :] = dot(assembled[near:, own:], far_image[own:, :]).astype(HALF)
    sums_of_own()

    def values_store():
        return pltpu.make_async_copy(values, values_out, store_sem.at[1])

    def take_near(sweep):
        for k in range(1, NEAR):
            level_copy(sweep, k).wait_recv()
        return levels[sweep, :NEAR].reshape(near, width)

    def sweep_once(sweep, carry):
        before = sweep - 1
        goes_on = sweep < ITERS - 1
        for k in range(NEAR, len(STENCIL)):
            level_copy(before, k).wait_recv()
        around = take_near(before)
        beyond = levels[before, NEAR:].reshape(-1, width)
        own_sums[...] += DAMPING * (dot(near_sums[...], around) + dot(far_sums[...], beyond))
        image[own:, :] += DAMPING * (
            dot(near_image[own:, :], around) + dot(far_image[own:, :], beyond)
        )
        margin = take_tiles(0, before)
        owed = own_sums[...] + dot(ghost_sums[...], margin)
        sums_src[sweep] = owed.astype(HALF).reshape(len(STENCIL), level, width)
        for k in OUTER_FIRST:
            sum_copy(sweep, k).start()
        send_tiles(1, sweep, image[own:, :] + dot(operator[own:, own:], margin))
        image[:own, :] += dot(operator[:own, own:], margin) + DAMPING * (
            dot(near_image[:own, :], around) + dot(far_image[:own, :], beyond)
        )
        total[:own, :] = target[...] - image[:own, :]
        pick_ahead(total[:own, :])
        values[...] += DAMPING * dot(psi[...], around)

        for k in range(1, len(STENCIL)):
            sum_copy(sweep, k).wait_recv()
        sums[sweep, 0] = sums_src[sweep, 0]
        send_restricted(sweep, first[...] - jnp.sum(sums[sweep].astype(F32), axis=0))
        returned = take_tiles(1, sweep)
        send_tiles(2, sweep, ahead[...] - dot(cross[...], returned))
        held[...] = (total[:own, :] - dot(spread[...], returned)).astype(HALF)
        total[...] = dot(inverse[:, :own], held[...])
        solve_part(sweep)
        arrived = take_tiles(2, sweep)
        send_tiles(3, sweep, total[own:, :] + dot(inverse[own:, own:], arrived))
        values[...] += DAMPING * (total[:own, :] + dot(inverse[:own, own:], arrived))

        @pl.when(goes_on)
        def _():
            pick_ahead(values[...])

        solve_rest(sweep, goes_on)

        returned = take_tiles(3, sweep)

        @pl.when(goes_on)
        def _():
            send_tiles(0, sweep, ahead[...] + DAMPING * dot(cross[...], returned))

        values[...] += DAMPING * dot(spread[...], returned)

        @pl.when(sweep == ITERS - 1)
        def _():
            values_store().start()

        @pl.when(goes_on)
        def _():
            image[...] = dot(operator[:, :own], values[...].astype(HALF))
            sums_of_own()

        return carry

    lax.fori_loop(1, ITERS, sweep_once, 0)
    around_ref[...] = take_near(ITERS - 1)
    psi_store.wait()
    values_store().wait()

    for d in range(tiles):
        basis_copy(d).wait_send()
        wide_copy(d).wait_send()

    def settle(sweep, carry):
        for d in range(tiles):
            tile_copy(2, sweep, d).wait_send()
            tile_copy(3, sweep, d).wait_send()
        for i in range(n_col - 1):
            block_copy(sweep, i).wait_send()
        for i in range(n_row - 1):
            part_copy(sweep, i).wait_send()
        for k in range(1, NEAR):
            level_copy(sweep, k).wait_send()

        @pl.when(sweep > 0)
        def _():
            for d in range(tiles):
                tile_copy(1, sweep, d).wait_send()
            for k in range(1, len(STENCIL)):
                sum_copy(sweep, k).wait_send()

        @pl.when(sweep < ITERS - 1)
        def _():
            for d in range(tiles):
                tile_copy(0, sweep, d).wait_send()
            for k in range(NEAR, len(STENCIL)):
                level_copy(sweep, k).wait_send()

        return carry

    lax.fori_loop(0, ITERS, settle, 0)


def finish(values_ref, psi_ref, around_ref, out_ref):
    out_ref[...] = values_ref[...] + DAMPING * dot(psi_ref[...], around_ref[...])


def solution(mesh):
    n_row, n_col = mesh.shape["row"], mesh.shape["col"]

    def per_device(
        right_side, local_operator, local_inverse, coarse_basis, coarse_inverse, send_rows, send_count
    ):
        target = right_side[0, 0]
        own, width = target.shape
        basis = coarse_basis[0, 0].T
        level, local = basis.shape
        rows_list = send_rows[0, 0]
        tiles, tile = rows_list.shape
        rim = tiles * tile
        coarse = coarse_inverse.reshape(-1, coarse_inverse.shape[2])
        points = len(STENCIL)
        near, far = NEAR * level, (points - NEAR) * level
        vmem = pl.BlockSpec(memory_space=pltpu.VMEM)
        anywhere = pl.BlockSpec(memory_space=pl.ANY)
        dma = pltpu.SemaphoreType.DMA
        values, psi, around = pl.pallas_call(
            functools.partial(kernel, n_row, n_col),
            out_shape=(
                jax.ShapeDtypeStruct((own, width), F32),
                jax.ShapeDtypeStruct((own, near), HALF),
                jax.ShapeDtypeStruct((near, width), HALF),
            ),
            in_specs=[
                anywhere, anywhere, anywhere, anywhere, anywhere, anywhere, anywhere,
            ],
            out_specs=(anywhere, anywhere, vmem),
            scratch_shapes=[
                pltpu.VMEM((local, local), HALF),
                pltpu.VMEM((local, local), HALF),
                pltpu.VMEM(coarse.shape, HALF),
                pltpu.VMEM((own, width), F32),
                pltpu.VMEM((level, local), HALF),
                pltpu.VMEM((tiles, tile), jnp.int32),
                pltpu.VMEM((1, tiles), jnp.int32),
                pltpu.VMEM((rim, own), HALF),
                pltpu.VMEM((own, rim), HALF),
                pltpu.VMEM((rim, rim), HALF),
                pltpu.VMEM((rim, width), F32),
                pltpu.VMEM((local, width), F32),
                pltpu.VMEM((local, width), F32),
                pltpu.VMEM((own, width), F32),
                pltpu.VMEM((own, width), HALF),
                pltpu.VMEM((level, width), F32),
                pltpu.VMEM((4, ITERS, tiles, tile, width), HALF),
                pltpu.VMEM((4, ITERS, tiles, tile, width), HALF),
                pltpu.VMEM((ITERS, level, width), HALF),
                pltpu.VMEM((ITERS, n_col, level, width), HALF),
                pltpu.VMEM((ITERS, n_row, level, width), HALF),
                pltpu.VMEM((ITERS, n_row, level, width), HALF),
                pltpu.VMEM((ITERS, points, level, width), HALF),
                pltpu.VMEM((ITERS, points, level, width), HALF),
                pltpu.VMEM((ITERS, points, level, width), HALF),
                pltpu.VMEM((tiles, level, tile), HALF),
                pltpu.VMEM((tiles, level, tile), HALF),
                pltpu.VMEM((tiles, near, tile), HALF),
                pltpu.VMEM((tiles, near, tile), HALF),
                pltpu.VMEM((near + far, local), HALF),
                pltpu.VMEM((own, near), HALF),
                pltpu.VMEM((local, near), HALF),
                pltpu.VMEM((local, far), HALF),
                pltpu.VMEM((near + far, rim), HALF),
                pltpu.VMEM((near + far, near), HALF),
                pltpu.VMEM((near + far, far), HALF),
                pltpu.VMEM((near + far, width), F32),
                dma((7,)),
                dma((2,)),
                dma((4, ITERS, tiles)),
                dma((4, ITERS, tiles)),
                dma((ITERS, n_col - 1)),
                dma((ITERS, n_col - 1)),
                dma((ITERS, n_row - 1)),
                dma((ITERS, n_row - 1)),
                dma((ITERS, points)),
                dma((ITERS, points)),
                dma((ITERS, points)),
                dma((ITERS, points)),
                dma((2, tiles)),
                dma((2, tiles)),
            ],
            compiler_params=pltpu.CompilerParams(
                collective_id=0, has_side_effects=True, vmem_limit_bytes=60 * 1024 * 1024
            ),
        )(
            target,
            local_operator[0, 0],
            local_inverse[0, 0],
            basis,
            coarse,
            rows_list,
            send_count[0],
        )
        rows = own // 2
        out = pl.pallas_call(
            finish,
            grid=(2,),
            out_shape=jax.ShapeDtypeStruct((own, width), F32),
            in_specs=[
                pl.BlockSpec((rows, width), lambda i: (i, 0)),
                pl.BlockSpec((rows, near), lambda i: (i, 0)),
                pl.BlockSpec((near, width), lambda i: (0, 0)),
            ],
            out_specs=pl.BlockSpec((rows, width), lambda i: (i, 0)),
        )(values, psi, around)
        return out[None, None]

    return jax.shard_map(
        per_device,
        mesh=mesh,
        in_specs=(
            P("row", "col", None, None),
            P("row", "col", None, None),
            P("row", "col", None, None),
            P("row", "col", None, None),
            P(None, "col", "row"),
            P("row", "col", None, None),
            P("row", "col", None),
        ),
        out_specs=P("row", "col", None, None),
        check_vma=False,
    )
```

```python
import functools

import jax
import jax.numpy as jnp
from jax import lax
from jax.experimental import pallas as pl
from jax.experimental.pallas import tpu as pltpu
from jax.sharding import PartitionSpec as P

ITERS = 3
DAMPING = 0.5
MESH = pl.DeviceIdType.MESH
OPPOSITE = (1, 0, 3, 2)
F32 = jnp.float32
HALF = jnp.bfloat16
STENCIL = (
    (0, 0), (-1, 0), (1, 0), (0, -1), (0, 1),
    (-2, 0), (2, 0), (-1, -1), (-1, 1), (1, -1), (1, 1), (0, -2), (0, 2),
)
NEAR = 5
OUTER_FIRST = (7, 8, 9, 10, 5, 6, 1, 2, 11, 12, 3, 4)


def stencil_index(down, right):
    return STENCIL.index((down, right))


def mirrored(k):
    return stencil_index(-STENCIL[k][0], -STENCIL[k][1])


def dot(left, right):
    return jnp.dot(left, right, preferred_element_type=F32)


def dot_turned(left, right):
    return lax.dot_general(left, right, (((1,), (1,)), ((), ())), preferred_element_type=F32)


def ring_steps(n_row, n_col):
    fast = 4
    half = n_col // 2
    rows = [(a, b) for a in range(n_row // fast) for b in range(fast)][1:]

    def row_hops(o):
        return 2 * min(o[0], n_row // fast - o[0]) + min(o[1], fast - o[1])

    cols = [(a, b, c) for a in range(2) for b in range(half // 2) for c in range(2)][1:]

    def col_hops(o):
        return o[0] + min(o[1], half // 2 - o[1])

    return sorted(rows, key=row_hops, reverse=True), sorted(cols, key=col_hops, reverse=True)


def kernel(
    n_row, n_col,
    target_hbm, operator_hbm, inverse_hbm, basis_hbm, coarse_hbm, rows_hbm, counts_hbm,
    values_out, psi_out, around_ref,
    operator, inverse, coarse, target, basis_ref, rows_ref, counts_ref, pick, spread, cross, ahead, total, image, values, held, first,
    packed, ghosts, gather_src, gathered, part_src, parts, sums_src, sums, levels,
    basis_src, basis_tiles, wide_src, wide_tiles, assembled, psi, near_image, far_image,
    ghost_sums, near_sums, far_sums, own_sums,
    load_sem, store_sem, pack_send, pack_recv, gather_send, gather_recv, part_send, part_recv,
    sums_send, sums_recv, level_send, level_recv, setup_send, setup_recv,
):
    own, width = target.shape
    tiles, tile = rows_ref.shape
    rim = tiles * tile
    level = basis_ref.shape[0]
    near = NEAR * level
    row = lax.axis_index("row")
    col = lax.axis_index("col")
    row_steps, col_steps = ring_steps(n_row, n_col)

    def at(down, right):
        return (
            lax.rem(row + (down + n_row), n_row) if down else row,
            lax.rem(col + (right + n_col), n_col) if right else col,
        )

    def row_peer(step):
        a, b = step
        return lax.rem(lax.div(row, 4) + a, n_row // 4) * 4 + lax.rem(lax.rem(row, 4) + b, 4)

    def col_peer(step):
        a, b, c = step
        quarter = n_col // 4
        return (
            lax.rem(lax.div(col, n_col // 2) + a, 2) * (n_col // 2)
            + lax.rem(lax.rem(lax.div(col, 2), quarter) + b, quarter) * 2
            + lax.rem(lax.rem(col, 2) + c, 2)
        )

    neighbours = [at(*STENCIL[1 + d]) for d in range(tiles)]

    loads = [
        pltpu.make_async_copy(source, place, load_sem.at[i])
        for i, (source, place) in enumerate(
            (
                (target_hbm, target),
                (inverse_hbm, inverse),
                (coarse_hbm, coarse),
                (operator_hbm, operator),
                (rows_hbm, rows_ref),
                (counts_hbm, counts_ref),
                (basis_hbm, basis_ref),
            )
        )
    ]
    for i in (4, 5, 0, 6, 1, 2, 3):
        loads[i].start()

    barrier = pltpu.get_barrier_semaphore()
    greeted = 0
    for step in row_steps:
        pl.semaphore_signal(barrier, inc=1, device_id=(row_peer(step), col), device_id_type=MESH)
        greeted += 1
    for step in col_steps:
        pl.semaphore_signal(barrier, inc=1, device_id=(row, col_peer(step)), device_id_type=MESH)
        greeted += 1
    for down, right in STENCIL:
        if down and right:
            pl.semaphore_signal(barrier, inc=1, device_id=at(down, right), device_id_type=MESH)
            greeted += 1

    def tile_copy(kind, sweep, d):
        return pltpu.make_async_remote_copy(
            src_ref=packed.at[kind, sweep, d],
            dst_ref=ghosts.at[kind, sweep, OPPOSITE[d]],
            send_sem=pack_send.at[kind, sweep, d],
            recv_sem=pack_recv.at[kind, sweep, OPPOSITE[d]],
            device_id=neighbours[d],
            device_id_type=MESH,
        )

    def store_tiles(kind, sweep, value):
        packed[kind, sweep] = value.astype(HALF).reshape(tiles, tile, width)

    def start_tiles(kind, sweep):
        for d in range(tiles):
            tile_copy(kind, sweep, d).start()

    def send_tiles(kind, sweep, value):
        store_tiles(kind, sweep, value)
        start_tiles(kind, sweep)

    def take_tiles(kind, sweep):
        for d in range(tiles):
            tile_copy(kind, sweep, d).wait_recv()
        return ghosts[kind, sweep].reshape(rim, width)

    def setup_copy(stage, source, place, d):
        return pltpu.make_async_remote_copy(
            src_ref=source.at[d],
            dst_ref=place.at[OPPOSITE[d]],
            send_sem=setup_send.at[stage, d],
            recv_sem=setup_recv.at[stage, OPPOSITE[d]],
            device_id=neighbours[d],
            device_id_type=MESH,
        )

    def basis_copy(d):
        return setup_copy(0, basis_src, basis_tiles, d)

    def wide_copy(d):
        return setup_copy(1, wide_src, wide_tiles, d)

    def block_copy(sweep, i):
        return pltpu.make_async_remote_copy(
            src_ref=gather_src.at[sweep],
            dst_ref=gathered.at[sweep, col],
            send_sem=gather_send.at[sweep, i],
            recv_sem=gather_recv.at[sweep, i],
            device_id=(row, col_peer(col_steps[i])),
            device_id_type=MESH,
        )

    def part_copy(sweep, i):
        peer = row_peer(row_steps[i])
        return pltpu.make_async_remote_copy(
            src_ref=part_src.at[sweep, peer],
            dst_ref=parts.at[sweep, row],
            send_sem=part_send.at[sweep, i],
            recv_sem=part_recv.at[sweep, i],
            device_id=(peer, col),
            device_id_type=MESH,
        )

    def sum_copy(sweep, k):
        return pltpu.make_async_remote_copy(
            src_ref=sums_src.at[sweep, k],
            dst_ref=sums.at[sweep, mirrored(k)],
            send_sem=sums_send.at[sweep, k],
            recv_sem=sums_recv.at[sweep, mirrored(k)],
            device_id=at(*STENCIL[k]),
            device_id_type=MESH,
        )

    def level_copy(sweep, k):
        return pltpu.make_async_remote_copy(
            src_ref=levels.at[sweep, 0],
            dst_ref=levels.at[sweep, mirrored(k)],
            send_sem=level_send.at[sweep, k],
            recv_sem=level_recv.at[sweep, mirrored(k)],
            device_id=at(*STENCIL[k]),
            device_id_type=MESH,
        )

    def send_restricted(sweep, value):
        restricted = value.astype(HALF)
        gather_src[sweep] = restricted
        gathered[sweep, col] = restricted
        for i in range(n_col - 1):
            block_copy(sweep, i).start()

    def solve_part(sweep):
        for i in range(n_col - 1):
            block_copy(sweep, i).wait_recv()
        part = dot(coarse[...], gathered[sweep].reshape(n_col * level, width)).astype(HALF)
        part_src[sweep] = part.reshape(n_row, level, width)
        for i in range(n_row - 1):
            part_copy(sweep, i).start()
        parts[sweep, row] = part_src[sweep, row]

    def solve_rest(sweep, far):
        for i in range(n_row - 1):
            part_copy(sweep, i).wait_recv()
        levels[sweep, 0] = jnp.sum(parts[sweep].astype(F32), axis=0).astype(HALF)

        def outer():
            for k in (7, 8, 9, 10, 5, 6, 11, 12):
                level_copy(sweep, k).start()

        if far is True:
            outer()
        else:
            pl.when(far)(outer)
        for k in range(1, NEAR):
            level_copy(sweep, k).start()

    def sums_of_own():
        own_sums[:near, :] = dot(assembled[:near, :], image[...].astype(HALF))
        own_sums[near:, :] = dot(assembled[near:, own:], image[own:, :].astype(HALF))

    def pick_ahead(value):
        coarser = value.astype(HALF)
        finer = (value - coarser.astype(F32)).astype(HALF)
        ahead[...] = dot(pick[...], coarser) + dot(pick[...], finer)

    place = lax.broadcasted_iota(jnp.int32, (1, tile), 1)
    square = lax.broadcasted_iota(jnp.int32, (tile, tile), 0) == lax.broadcasted_iota(
        jnp.int32, (tile, tile), 1
    )
    loads[4].wait()
    loads[5].wait()
    lists = [
        jnp.where(place < counts_ref[:, d : d + 1], rows_ref[d : d + 1, :], -1).astype(F32)
        for d in range(tiles)
    ]
    along = lax.broadcasted_iota(jnp.int32, (tile, own), 1).astype(F32)
    for d in range(tiles):
        upright = jnp.sum(
            jnp.where(square, jnp.broadcast_to(lists[d], (tile, tile)), 0.0), axis=1, keepdims=True
        )
        pick[d * tile : (d + 1) * tile, :] = jnp.where(along == upright, 1.0, 0.0).astype(HALF)
    loads[6].wait()
    for d in range(tiles):
        basis_src[d] = basis_ref[:, own + d * tile : own + (d + 1) * tile]
    loads[0].wait()
    held[...] = target[...].astype(HALF)
    store_tiles(2, 0, dot(pick[...], held[...]))

    pl.semaphore_wait(barrier, greeted)

    start_tiles(2, 0)
    for d in range(tiles):
        basis_copy(d).start()
    down = lax.broadcasted_iota(jnp.int32, (own, tile), 0).astype(F32)
    for d in range(tiles):
        spread[:, d * tile : (d + 1) * tile] = jnp.where(down == lists[d], 1.0, 0.0).astype(HALF)
    cross[...] = dot(pick[...], spread[...]).astype(HALF)
    assembled[...] = jnp.zeros_like(assembled)
    coarse_own = dot(basis_ref[:, :own], held[...])
    loads[1].wait()
    total[...] = dot(inverse[:, :own], held[...])
    margin = take_tiles(2, 0)
    first[...] = coarse_own + dot(basis_ref[:, own:], margin)
    send_restricted(0, first[...])
    send_tiles(3, 0, total[own:, :] + dot(inverse[own:, own:], margin))
    total[:own, :] += dot(inverse[:own, own:], margin)

    assembled[:level, :own] = basis_ref[:, :own]
    for d in range(tiles):
        basis_copy(d).wait_recv()
    for d in range(tiles):
        assembled[(1 + d) * level : (2 + d) * level, :own] = dot(
            basis_tiles[d], pick[d * tile : (d + 1) * tile, :]
        ).astype(HALF)
    wide = dot(assembled[:near, :own], spread[...]).astype(HALF)
    for d in range(tiles):
        wide_src[d] = wide[:, d * tile : (d + 1) * tile]
    for d in range(tiles):
        wide_copy(d).start()

    loads[2].wait()
    solve_part(0)
    values[...] = DAMPING * total[:own, :]
    pick_ahead(values[...])
    returned = take_tiles(3, 0)
    send_tiles(0, 0, ahead[...] + DAMPING * dot(cross[...], returned))
    values[...] += DAMPING * dot(spread[...], returned)
    held[...] = values[...].astype(HALF)
    loads[3].wait()
    image[...] = dot(operator[:, :own], held[...])
    psi[...] = assembled[:near, :own].astype(F32).T.astype(HALF)
    psi_store = pltpu.make_async_copy(psi, psi_out, store_sem.at[0])
    psi_store.start()
    for d in range(tiles):
        wide_copy(d).wait_recv()
    for d in range(tiles):
        for e in range(NEAR):
            k = stencil_index(
                STENCIL[1 + d][0] + STENCIL[e][0], STENCIL[1 + d][1] + STENCIL[e][1]
            )
            assembled[k * level : (k + 1) * level, own + d * tile : own + (d + 1) * tile] = (
                wide_tiles[d, e * level : (e + 1) * level, :]
            )
    solve_rest(0, True)
    near_image[...] = dot_turned(operator[...], assembled[:near, :]).astype(HALF)
    far_image[...] = dot_turned(operator[:, own:], assembled[near:, own:]).astype(HALF)
    ghost_sums[:near, :] = dot(assembled[:near, :], operator[:, own:]).astype(HALF)
    ghost_sums[near:, :] = dot(assembled[near:, own:], operator[own:, own:]).astype(HALF)
    near_sums[:near, :] = dot(assembled[:near, :], near_image[...]).astype(HALF)
    near_sums[near:, :] = dot(assembled[near:, own:], near_image[own:, :]).astype(HALF)
    far_sums[:near, :] = dot(assembled[:near, :], far_image[...]).astype(HALF)
    far_sums[near:, :] = dot(assembled[near:, own:], far_image[own:, :]).astype(HALF)
    sums_of_own()

    def values_store():
        return pltpu.make_async_copy(values, values_out, store_sem.at[1])

    def take_near(sweep):
        for k in range(1, NEAR):
            level_copy(sweep, k).wait_recv()
        return levels[sweep, :NEAR].reshape(near, width)

    def sweep_once(sweep, carry):
        before = sweep - 1
        goes_on = sweep < ITERS - 1
        for k in range(NEAR, len(STENCIL)):
            level_copy(before, k).wait_recv()
        around = take_near(before)
        beyond = levels[before, NEAR:].reshape(-1, width)
        own_sums[...] += DAMPING * (dot(near_sums[...], around) + dot(far_sums[...], beyond))
        image[own:, :] += DAMPING * (
            dot(near_image[own:, :], around) + dot(far_image[own:, :], beyond)
        )
        margin = take_tiles(0, before)
        owed = own_sums[...] + dot(ghost_sums[...], margin)
        sums_src[sweep] = owed.astype(HALF).reshape(len(STENCIL), level, width)
        for k in OUTER_FIRST:
            sum_copy(sweep, k).start()
        send_tiles(1, sweep, image[own:, :] + dot(operator[own:, own:], margin))
        image[:own, :] += dot(operator[:own, own:], margin) + DAMPING * (
            dot(near_image[:own, :], around) + dot(far_image[:own, :], beyond)
        )
        total[:own, :] = target[...] - image[:own, :]
        pick_ahead(total[:own, :])
        values[...] += DAMPING * dot(psi[...], around)

        for k in range(1, len(STENCIL)):
            sum_copy(sweep, k).wait_recv()
        sums[sweep, 0] = sums_src[sweep, 0]
        send_restricted(sweep, first[...] - jnp.sum(sums[sweep].astype(F32), axis=0))
        returned = take_tiles(1, sweep)
        send_tiles(2, sweep, ahead[...] - dot(cross[...], returned))
        held[...] = (total[:own, :] - dot(spread[...], returned)).astype(HALF)
        total[...] = dot(inverse[:, :own], held[...])
        solve_part(sweep)
        arrived = take_tiles(2, sweep)
        send_tiles(3, sweep, total[own:, :] + dot(inverse[own:, own:], arrived))
        values[...] += DAMPING * (total[:own, :] + dot(inverse[:own, own:], arrived))

        @pl.when(goes_on)
        def _():
            pick_ahead(values[...])

        solve_rest(sweep, goes_on)

        returned = take_tiles(3, sweep)

        @pl.when(goes_on)
        def _():
            send_tiles(0, sweep, ahead[...] + DAMPING * dot(cross[...], returned))

        values[...] += DAMPING * dot(spread[...], returned)

        @pl.when(sweep == ITERS - 1)
        def _():
            values_store().start()

        @pl.when(goes_on)
        def _():
            image[...] = dot(operator[:, :own], values[...].astype(HALF))
            sums_of_own()

        return carry

    lax.fori_loop(1, ITERS, sweep_once, 0)
    around_ref[...] = take_near(ITERS - 1)
    psi_store.wait()
    values_store().wait()

    for d in range(tiles):
        basis_copy(d).wait_send()
        wide_copy(d).wait_send()

    def settle(sweep, carry):
        for d in range(tiles):
            tile_copy(2, sweep, d).wait_send()
            tile_copy(3, sweep, d).wait_send()
        for i in range(n_col - 1):
            block_copy(sweep, i).wait_send()
        for i in range(n_row - 1):
            part_copy(sweep, i).wait_send()
        for k in range(1, NEAR):
            level_copy(sweep, k).wait_send()

        @pl.when(sweep > 0)
        def _():
            for d in range(tiles):
                tile_copy(1, sweep, d).wait_send()
            for k in range(1, len(STENCIL)):
                sum_copy(sweep, k).wait_send()

        @pl.when(sweep < ITERS - 1)
        def _():
            for d in range(tiles):
                tile_copy(0, sweep, d).wait_send()
            for k in range(NEAR, len(STENCIL)):
                level_copy(sweep, k).wait_send()

        return carry

    lax.fori_loop(0, ITERS, settle, 0)


def finish(values_ref, psi_ref, around_ref, out_ref):
    out_ref[...] = values_ref[...] + DAMPING * dot(psi_ref[...], around_ref[...])


def solution(mesh):
    n_row, n_col = mesh.shape["row"], mesh.shape["col"]

    def per_device(
        right_side, local_operator, local_inverse, coarse_basis, coarse_inverse, send_rows, send_count
    ):
        target = right_side[0, 0]
        own, width = target.shape
        basis = coarse_basis[0, 0].T
        level, local = basis.shape
        rows_list = send_rows[0, 0]
        tiles, tile = rows_list.shape
        rim = tiles * tile
        coarse = coarse_inverse.reshape(-1, coarse_inverse.shape[2])
        points = len(STENCIL)
        near, far = NEAR * level, (points - NEAR) * level
        vmem = pl.BlockSpec(memory_space=pltpu.VMEM)
        anywhere = pl.BlockSpec(memory_space=pl.ANY)
        dma = pltpu.SemaphoreType.DMA
        values, psi, around = pl.pallas_call(
            functools.partial(kernel, n_row, n_col),
            out_shape=(
                jax.ShapeDtypeStruct((own, width), F32),
                jax.ShapeDtypeStruct((own, near), HALF),
                jax.ShapeDtypeStruct((near, width), HALF),
            ),
            in_specs=[
                anywhere, anywhere, anywhere, anywhere, anywhere, anywhere, anywhere,
            ],
            out_specs=(anywhere, anywhere, vmem),
            scratch_shapes=[
                pltpu.VMEM((local, local), HALF),
                pltpu.VMEM((local, local), HALF),
                pltpu.VMEM(coarse.shape, HALF),
                pltpu.VMEM((own, width), F32),
                pltpu.VMEM((level, local), HALF),
                pltpu.VMEM((tiles, tile), jnp.int32),
                pltpu.VMEM((1, tiles), jnp.int32),
                pltpu.VMEM((rim, own), HALF),
                pltpu.VMEM((own, rim), HALF),
                pltpu.VMEM((rim, rim), HALF),
                pltpu.VMEM((rim, width), F32),
                pltpu.VMEM((local, width), F32),
                pltpu.VMEM((local, width), F32),
                pltpu.VMEM((own, width), F32),
                pltpu.VMEM((own, width), HALF),
                pltpu.VMEM((level, width), F32),
                pltpu.VMEM((4, ITERS, tiles, tile, width), HALF),
                pltpu.VMEM((4, ITERS, tiles, tile, width), HALF),
                pltpu.VMEM((ITERS, level, width), HALF),
                pltpu.VMEM((ITERS, n_col, level, width), HALF),
                pltpu.VMEM((ITERS, n_row, level, width), HALF),
                pltpu.VMEM((ITERS, n_row, level, width), HALF),
                pltpu.VMEM((ITERS, points, level, width), HALF),
                pltpu.VMEM((ITERS, points, level, width), HALF),
                pltpu.VMEM((ITERS, points, level, width), HALF),
                pltpu.VMEM((tiles, level, tile), HALF),
                pltpu.VMEM((tiles, level, tile), HALF),
                pltpu.VMEM((tiles, near, tile), HALF),
                pltpu.VMEM((tiles, near, tile), HALF),
                pltpu.VMEM((near + far, local), HALF),
                pltpu.VMEM((own, near), HALF),
                pltpu.VMEM((local, near), HALF),
                pltpu.VMEM((local, far), HALF),
                pltpu.VMEM((near + far, rim), HALF),
                pltpu.VMEM((near + far, near), HALF),
                pltpu.VMEM((near + far, far), HALF),
                pltpu.VMEM((near + far, width), F32),
                dma((7,)),
                dma((2,)),
                dma((4, ITERS, tiles)),
                dma((4, ITERS, tiles)),
                dma((ITERS, n_col - 1)),
                dma((ITERS, n_col - 1)),
                dma((ITERS, n_row - 1)),
                dma((ITERS, n_row - 1)),
                dma((ITERS, points)),
                dma((ITERS, points)),
                dma((ITERS, points)),
                dma((ITERS, points)),
                dma((2, tiles)),
                dma((2, tiles)),
            ],
            compiler_params=pltpu.CompilerParams(
                collective_id=0, has_side_effects=True, vmem_limit_bytes=60 * 1024 * 1024
            ),
        )(
            target,
            local_operator[0, 0],
            local_inverse[0, 0],
            basis,
            coarse,
            rows_list,
            send_count[0],
        )
        rows = own // 2
        out = pl.pallas_call(
            finish,
            grid=(2,),
            out_shape=jax.ShapeDtypeStruct((own, width), F32),
            in_specs=[
                pl.BlockSpec((rows, width), lambda i: (i, 0)),
                pl.BlockSpec((rows, near), lambda i: (i, 0)),
                pl.BlockSpec((near, width), lambda i: (0, 0)),
            ],
            out_specs=pl.BlockSpec((rows, width), lambda i: (i, 0)),
        )(values, psi, around)
        return out[None, None]

    return jax.shard_map(
        per_device,
        mesh=mesh,
        in_specs=(
            P("row", "col", None, None),
            P("row", "col", None, None),
            P("row", "col", None, None),
            P("row", "col", None, None),
            P(None, "col", "row"),
            P("row", "col", None, None),
            P("row", "col", None),
        ),
        out_specs=P("row", "col", None, None),
        check_vma=False,
    )
```
